32 devices in a mesh: shot: 2 (over x), freq: 16 (over z, y, core).
Axes of the slice: x: 2, y: 2, z: 4, core: 2. Of those that a mesh axis runs over, the one named last changes fastest.
Arguments:
- receiver_data: float32 [64, 2, 32, 1024], P(('shot', 'freq')), parts along dimension 0, may hold values from -6 to 6
- source_spectrum: float32 [32, 2], P('freq'), may hold values from -4 to 4
- filter_taps: float32 [32, 4, 6], P('freq'), may hold values from -1.5 to 1.5, as said below
- slowness: float32 [16, 32, 1024], P('freq'), may hold values from 0.5 to 2
- depth_owner: int32 [6], P('shot'), parts along dimension 0, may hold values from 0 to 15
- source_position: int32 [4], P('shot'), parts along dimension 0, may hold values from 0 to 31
Outputs:
- migrated_image: float32 [32, 32, 1024], P(('shot', 'freq')), parts along dimension 0
The draws below stay inside these ranges and needn't reach their ends.
There are 2 independent parts, one for each index of `shot`. The reference program is written for one: setup_inputs(seed, part) draws one part's arguments, and reference() takes and returns one part's arrays. A program takes and returns all parts, laid end to end along the dimension named above; an argument that names none is the same for every part. Nothing has to cross between parts.
Inputs may be any that keep to these rules, and one draw needn't show every extreme that they name: `filter_taps`: each frequency and direction holds three complex taps.
All inputs are finite; a program needn't handle non-finite values.
Results may differ from the reference program's by a relative error of at most 0.0001.
Values sent between devices are 32-bit elements; how exact they have to be, the bound alone decides.
A program may use at most 64 MiB of HBM per device.

```python
import math
import jax
import jax.numpy as jnp
from jax import lax

NX = 32
NY = 1024
STEPS = 3
NF = 32
SLABS = 16


def draw_filter_taps(key, part):
    keys = jax.random.split(jax.random.fold_in(key, 17), 5)
    shape = (NF, 4)
    angles = jax.random.uniform(keys[0], shape, jnp.float32, -math.pi, math.pi)
    first_re = jax.random.uniform(keys[1], shape, jnp.float32, 0.04, 0.1)
    first_im = jax.random.uniform(keys[2], shape, jnp.float32, -0.1, 0.1)
    second_re = jax.random.uniform(keys[3], shape, jnp.float32, 0.02, 0.04)
    second_im = jax.random.uniform(keys[4], shape, jnp.float32, -0.04, 0.04)
    rot_re = jnp.cos(angles)
    rot_im = jnp.sin(angles)
    inner_re = rot_re * first_re - rot_im * first_im
    inner_im = rot_re * first_im + rot_im * first_re
    outer_re = rot_re * second_re - rot_im * second_im
    outer_im = rot_re * second_im + rot_im * second_re
    centre_re = rot_re - 2.0 * inner_re - 2.0 * outer_re
    centre_im = rot_im - 2.0 * inner_im - 2.0 * outer_im
    return jnp.stack([centre_re, centre_im, inner_re, inner_im, outer_re, outer_im], axis=-1).astype(jnp.float32)


def levels(rng, shape, shards, low, high):
    def one(dim, parts):
        steps = jax.random.uniform(jax.random.fold_in(jax.random.fold_in(rng, 6), dim), (parts,), jnp.float32, low / len(shards), high / len(shards))
        return jnp.repeat(jnp.exp(steps), shape[dim] // parts).reshape((-1,) + (1,) * (len(shape) - dim - 1))

    factor_of = one(*shards[0])
    for cut in shards[1:]:
        factor_of = factor_of * one(*cut)
    return factor_of


def gaussian(rng, dims, spread, most, cuts=(), kind=jnp.bfloat16):
    drawn = spread * jax.random.normal(rng, dims, jnp.float32)
    if cuts:
        drawn = drawn * levels(rng, dims, cuts, -0.22, 0.18)
    return jnp.clip(drawn, -most, most).astype(kind)


def setup_inputs(seed: int = 0, part: int = 0) -> dict:
    splits = jax.random.split(jax.random.key(seed), 7)
    own_keys = jax.random.split(jax.random.fold_in(splits[6], part), 7)
    receiver_data = gaussian(own_keys[0], (NF, 2, NX, NY), 1.0, 6.0, ((0, 16),), jnp.float32)
    source_spectrum = gaussian(splits[1], (NF, 2), 1.0, 4.0, ((0, 16),), jnp.float32)
    filter_taps = draw_filter_taps(jax.random.fold_in(splits[6], 71), part)
    slowness = jnp.clip(jnp.exp(math.log(2.0) - 1.3862944 * jax.random.uniform(splits[3], (SLABS, NX, NY), jnp.float32) ** levels(splits[3], (SLABS, NX, NY), ((0, 16),), -0.2, 0.2)), 0.5, 2.0)
    depth_owner = jax.random.randint(own_keys[4], (STEPS,), 0, SLABS).astype(jnp.int32)
    source_position = jax.random.randint(own_keys[5], (2,), 0, NX).astype(jnp.int32)
    return {"receiver_data": receiver_data, "source_spectrum": source_spectrum, "filter_taps": filter_taps, "slowness": slowness, "depth_owner": depth_owner, "source_position": source_position}


lens_rate = 3.0
wave_rate = 0.5
directions = ((1, 0), (0, 1), (1, 1), (1, -1))

def source_start(spectrum, position, freq_index, freq_total, height, breadth):
    src_row = position[0].astype(jnp.float32)
    src_col = position[1].astype(jnp.float32)
    row_axis = jnp.arange(height, dtype=jnp.float32)[:, None]
    col_axis = jnp.arange(breadth, dtype=jnp.float32)[None, :]
    distance = jnp.sqrt((row_axis - src_row) ** 2 + (col_axis - src_col) ** 2 + 1.0)
    amplitude = 1.0 / (1.0 + distance / (height / 4.0))
    wavenumber = (freq_index.astype(jnp.float32) + 1.0) * (wave_rate / freq_total)
    phase_map = wavenumber[:, None, None] * distance[None]
    base_re = amplitude[None] * jnp.cos(phase_map)
    base_im = -amplitude[None] * jnp.sin(phase_map)
    wave_re = spectrum[:, 0][:, None, None]
    wave_im = spectrum[:, 1][:, None, None]
    return jnp.stack([wave_re * base_re - wave_im * base_im, wave_re * base_im + wave_im * base_re], axis=1)

def complex_mul(values, coef_re, coef_im):
    coef_re = coef_re[:, None, None]
    coef_im = coef_im[:, None, None]
    return jnp.stack([values[:, 0] * coef_re - values[:, 1] * coef_im, values[:, 0] * coef_im + values[:, 1] * coef_re], axis=1)

def thin_lens(wavefield, layer_slab, freq_index, freq_total, handed):
    phases = (freq_index.astype(jnp.float32) + 1.0)[:, None, None] * (lens_rate / freq_total) * layer_slab[None]
    rot_re = jnp.cos(phases)
    rot_im = handed * jnp.sin(phases)
    part_re = wavefield[:, 0]
    part_im = wavefield[:, 1]
    return jnp.stack([part_re * rot_re - part_im * rot_im, part_re * rot_im + part_im * rot_re], axis=1)

def directional(wavefield, coeffs, step_x, step_y, handed):
    height = wavefield.shape[2]
    breadth = wavefield.shape[3]
    padded = jnp.pad(wavefield, ((0, 0), (0, 0), (2, 2), (2, 2)))

    def adjacent(offset):
        return padded[:, :, 2 + offset * step_x:2 + offset * step_x + height, 2 + offset * step_y:2 + offset * step_y + breadth]
    inner_pair = adjacent(1) + adjacent(-1)
    outer_pair = adjacent(2) + adjacent(-2)
    result = complex_mul(wavefield, coeffs[:, 0], handed * coeffs[:, 1])
    result = result + complex_mul(inner_pair, coeffs[:, 2], handed * coeffs[:, 3])
    return result + complex_mul(outer_pair, coeffs[:, 4], handed * coeffs[:, 5])

def depth_step(source, receiver, layer_slab, filter_taps, freq_index, freq_total):
    source = thin_lens(source, layer_slab, freq_index, freq_total, -1.0)
    receiver = thin_lens(receiver, layer_slab, freq_index, freq_total, 1.0)
    for direction, (step_x, step_y) in enumerate(directions):
        source = directional(source, filter_taps[:, direction], step_x, step_y, 1.0)
        receiver = directional(receiver, filter_taps[:, direction], step_x, step_y, -1.0)
    return (source, receiver)

def reference(receiver_data, source_spectrum, filter_taps, slowness, depth_owner, source_position):
    freq_index = jnp.arange(NF, dtype=jnp.int32)
    source = source_start(source_spectrum, source_position, freq_index, NF, NX, NY)
    receiver = receiver_data
    slab_ids = jnp.arange(SLABS, dtype=jnp.int32)
    migrated = jnp.zeros((SLABS, NX, NY), jnp.float32)
    for level in range(STEPS):
        layer_slab = lax.dynamic_index_in_dim(slowness, depth_owner[level].astype(jnp.int32), 0, keepdims=False)
        source, receiver = depth_step(source, receiver, layer_slab, filter_taps, freq_index, NF)
        correlation = lax.optimization_barrier(jnp.sum(source[:, 0] * receiver[:, 0] + source[:, 1] * receiver[:, 1], axis=0)) / math.sqrt(NF)
        owner_mask = (slab_ids == depth_owner[level]).astype(jnp.float32)
        migrated = migrated + owner_mask[:, None, None] * correlation[None]
    return migrated
```

```python
import functools
import math

import jax
import jax.numpy as jnp
from jax import lax
from jax.experimental import pallas as pl
from jax.experimental.pallas import tpu as pltpu
from jax.sharding import PartitionSpec as P

lens_rate = 3.0
wave_rate = 0.5
middle = 1.25
MESH = pl.DeviceIdType.MESH
SUB = 8
LANE = 128
TOP = 8


def sincos(x):
    k = jnp.floor(x * (2.0 / math.pi) + 0.5)
    r = x - k * 1.5703125
    r = r - k * 4.837512969970703125e-4
    r = r - k * 7.54978995489188216e-8
    q = k.astype(jnp.int32)
    z = r * r
    s = r + r * z * (-1.6666654611e-1 + z * (8.3321608736e-3 - z * 1.9515295891e-4))
    c = 1.0 - 0.5 * z + z * z * (
        4.166664568298827e-2 + z * (-1.388731625493765e-3 + z * 2.443315711809948e-5)
    )
    swap = (q & 1) == 1
    sin = jnp.where(swap, c, s)
    cos = jnp.where(swap, s, c)
    sin = jnp.where((q & 2) == 2, -sin, sin)
    cos = jnp.where(((q + 1) & 2) == 2, -cos, cos)
    return sin, cos


def small_sincos(h):
    z = h * h
    s = h * (1.0 + z * (-1.0 / 6 + z * (1.0 / 120 + z * (-1.0 / 5040 + z * (1.0 / 362880)))))
    c = 1.0 + z * (-0.5 + z * (1.0 / 24 + z * (-1.0 / 720 + z * (1.0 / 40320 + z * (-1.0 / 3628800)))))
    t = s + s
    return t * c, 1.0 - t * s


def lane_index():
    return lax.broadcasted_iota(jnp.int32, (SUB, LANE), 1)


def butterfly(tiles):
    tiles = list(tiles)
    lanes = lane_index()
    step = 1
    while step < len(tiles):
        low = (lanes & step) == 0
        for v in range(len(tiles)):
            if v & step == 0:
                a, b = tiles[v], tiles[v + step]
                tiles[v] = jnp.where(low, a, pltpu.roll(b, step, 1))
                tiles[v + step] = jnp.where(low, pltpu.roll(a, LANE - step, 1), b)
        step *= 2
    return tiles


def pieces(cr, nb, rt, cb):
    row = cb * SUB
    size = min(cr, SUB)
    return [(rt * (nb * SUB // cr) + (row + o) // cr, (row + o) % cr, size, o) for o in range(0, SUB, size)]


def tile_load(ref, nb, rt, cb):
    got = [ref[c, r : r + m] for c, r, m, _ in pieces(ref.shape[1], nb, rt, cb)]
    return got[0] if len(got) == 1 else jnp.concatenate(got, axis=0)


def tile_store(ref, nb, rt, cb, value):
    for c, r, m, o in pieces(ref.shape[1], nb, rt, cb):
        ref[c, r : r + m] = value[o : o + m]


def kernel(
    n,
    owner_hbm,
    position_hbm,
    spectrum_hbm,
    taps_hbm,
    recv_hbm,
    slow,
    out,
    owner,
    position,
    spectrum,
    taps,
    small_sem,
    rbuf,
    fx,
    fy,
    coefs,
    turns,
    slab,
    all_slow,
    slabs,
    parts,
    near,
    red,
    image,
    load_sem,
    own_sem,
    a_send,
    a_recv,
    b_send,
    b_recv,
    pass_send,
    pass_recv,
    near_send,
    near_recv,
    c_send,
    c_recv,
    d_send,
    d_recv,
):
    me = lax.axis_index("freq")
    steps = owner.shape[0]
    fl = rbuf.shape[0]
    height = rbuf.shape[2]
    breadth = rbuf.shape[3]
    nb = breadth // LANE
    nrt = height // SUB
    freq_total = n * fl
    first = me * fl

    def peer(i):
        if n & (n - 1):
            return lax.rem(me + i, n)
        to = 0
        for b in range(n.bit_length() - 1):
            bit = lax.rem(lax.div(me, 1 << b), 2)
            to = to + (1 << b) * (1 - bit if i >> b & 1 else bit)
        return to

    partners = [peer(i) for i in range(n)]
    rounds = range(n - 1, 0, -1)
    alike = range(n - 2, 0, -2)
    chips = n // 2
    side = lax.rem(me, 2)
    chip = lax.div(me, 2)
    mate = partners[1]

    def place(device):
        return lax.rem(device, 2) * chips + lax.div(device, 2)

    mine = place(me)
    own_half = pl.ds(side * chips, chips)
    other_half = pl.ds((1 - side) * chips, chips)

    def remote(src, dst, send, recv, to):
        return pltpu.make_async_remote_copy(
            src_ref=src, dst_ref=dst, send_sem=send, recv_sem=recv,
            device_id={"freq": to}, device_id_type=MESH,
        )

    barrier = pltpu.get_barrier_semaphore()
    for i in rounds:
        pl.semaphore_signal(barrier, inc=1, device_id={"freq": partners[i]}, device_id_type=MESH)
    load = pltpu.make_async_copy(recv_hbm, rbuf, load_sem)
    load.start()
    small = [
        pltpu.make_async_copy(src, dst, small_sem.at[j])
        for j, (src, dst) in enumerate(
            ((owner_hbm, owner), (position_hbm, position), (spectrum_hbm, spectrum), (taps_hbm, taps))
        )
    ]
    for copy in small:
        copy.start()
    pl.semaphore_wait(barrier, n - 1)

    a_copies = [
        remote(slow.at[place(partners[i])], all_slow.at[me], a_send.at[i], a_recv.at[i], partners[i])
        for i in rounds
    ]
    for copy in a_copies:
        copy.start()
    own = pltpu.make_async_copy(slow.at[mine], all_slow.at[me], own_sem)
    own.start()

    def rows(rt, k=0):
        start = TOP + rt * SUB + k
        return slice(start, start + SUB)

    lanes = lane_index()
    zero = jnp.zeros((SUB, LANE), jnp.float32)

    @pl.loop(0, fl * 2)
    def _(field):
        for part in range(2):
            for cx in range(nb + 4):
                for buf in (fx, fy):
                    buf[field, part, cx, 0:TOP] = zero
                    buf[field, part, cx, TOP + height : 2 * TOP + height] = zero

    for copy in small:
        copy.wait()

    @pl.loop(0, fl)
    def _(f):
        half = jnp.broadcast_to(((first + f).astype(jnp.float32) + 1.0) * (lens_rate / freq_total * 0.5), (SUB, LANE))
        sin, cos = sincos(half * (2.0 * middle))
        turn_re, turn_im = cos, -sin
        for d in range(4):
            c = [jnp.broadcast_to(taps[f, d, j], (SUB, LANE)) for j in range(6)]
            m = jnp.maximum(jnp.abs(c[0]), jnp.abs(c[1]))
            some = m > 0.0
            inverse = 1.0 / jnp.where(some, m, 1.0)
            ur = jnp.where(some, c[0] * inverse, 1.0)
            ui = jnp.where(some, c[1] * inverse, 0.0)
            q = ur * ur + ui * ui
            root = 1.0 / jnp.sqrt(q)
            root = root * (1.5 - 0.5 * q * root * root)
            pr = ur * root
            pi = ui * root
            turn_re, turn_im = turn_re * pr - turn_im * pi, turn_re * pi + turn_im * pr
            coefs[f, d, 0] = m * (q * root)
            for j in (1, 3):
                coefs[f, d, j] = c[j + 1] * pr + c[j + 2] * pi
                coefs[f, d, j + 1] = c[j + 2] * pr - c[j + 1] * pi
        turns[f, 0] = half
        turns[f, 1] = half * middle
        turns[f, 2] = turn_re
        turns[f, 3] = turn_im

    src_row = position[0].astype(jnp.float32)
    src_col = position[1].astype(jnp.float32)
    subs = lax.broadcasted_iota(jnp.int32, (SUB, LANE), 0)
    across = (lanes & (nb - 1)) * LANE + (lanes - (lanes & (nb - 1)))

    @pl.loop(0, nrt)
    def _(rt):
        row = (subs + rt * SUB).astype(jnp.float32) - src_row
        at = pl.ds(pl.multiple_of(TOP + rt * SUB, SUB), SUB)
        for cb in range(nb):
            col = (across + cb).astype(jnp.float32) - src_col
            distance = jnp.sqrt(row * row + col * col + 1.0)
            amplitude = 1.0 / (1.0 + distance / (height / 4.0))
            for f in range(fl):
                number = ((first + f).astype(jnp.float32) + 1.0) * (wave_rate / freq_total)
                sin, cos = sincos(number * distance)
                base_re = amplitude * cos
                base_im = -amplitude * sin
                wr = spectrum[f, 0]
                wi = spectrum[f, 1]
                fx[2 * f, 0, cb + 2, at] = wr * base_re - wi * base_im
                fx[2 * f, 1, cb + 2, at] = wr * base_im + wi * base_re

    load.wait()

    @pl.loop(0, fl)
    def _(f):
        for part in range(2):
            for rt in range(nrt):
                tiles = butterfly(
                    [rbuf[f, part, rt * SUB : rt * SUB + SUB, v * LANE : v * LANE + LANE] for v in range(nb)]
                )
                for cb in range(nb):
                    fx[2 * f + 1, part, cb + 2, rows(rt)] = tiles[cb] if part == 0 else -tiles[cb]

    own.wait()
    for copy in a_copies:
        copy.wait_recv()
    b_copies = []
    passes = []
    for t in range(steps):
        slabs[t, mine] = all_slow[owner[t]]
        b_copies.append(
            [
                remote(slabs.at[t, mine], slabs.at[t, mine], b_send.at[t, i], b_recv.at[t, i], partners[i])
                for i in alike
            ]
        )
        passes.append(remote(slabs.at[t, own_half], slabs.at[t, own_half], pass_send.at[t], pass_recv.at[t], mate))

    def begin(copies):
        for copy in copies:
            copy.start()

    def left(copies):
        for copy in copies:
            copy.wait_send()

    def hand_on(t):
        for copy in b_copies[t]:
            copy.wait_recv()
        passes[t].start()

    begin(b_copies[0])
    for t in range(1, steps):
        left(b_copies[t - 1])
        begin(b_copies[t])
    hand_on(0)

    def after(x):
        moved = jnp.where(lanes < LANE - nb, pltpu.roll(x, LANE - nb, 1), pltpu.roll(x, LANE - nb - 1, 1))
        return jnp.where(lanes == LANE - 1, 0.0, moved)

    def before(x):
        moved = jnp.where(lanes >= nb, pltpu.roll(x, nb, 1), pltpu.roll(x, nb + 1, 1))
        return jnp.where(lanes == 0, 0.0, moved)

    def combine(c, x, one, two):
        (xr, xi), (pr, pi), (qr, qi) = x, one, two
        re = c[0] * xr + (c[1] * pr - c[2] * pi) + (c[3] * qr - c[4] * qi)
        im = c[0] * xi + (c[1] * pi + c[2] * pr) + (c[3] * qi + c[4] * qr)
        return re, im

    def coefficients(f, d):
        return [coefs[f, d, j] for j in range(5)]

    def around(got, p):
        whole = {cb: got[cb][p] for cb in range(nb)}
        for k in range(2):
            whole[nb + k] = after(got[k][p])
            whole[k - 2] = before(got[nb - 2 + k][p])
        return whole

    def put(dst, field, rt, got):
        for p in range(2):
            whole = around(got, p)
            for cb in range(-2, nb + 2):
                dst[field, p, cb + 2, rows(rt)] = whole[cb]

    def lens(slow_now, src, dst):
        for rt in range(nrt):
            tiles = butterfly([tile_load(slow_now, nb, rt, v) for v in range(nb)])
            for cb in range(nb):
                slab[cb, rt * SUB : rt * SUB + SUB] = tiles[cb]

        @pl.loop(0, fl)
        def _(f):
            half, shift, turn_re, turn_im = (turns[f, j] for j in range(4))
            for rt in range(nrt):
                for cb in range(nb):
                    sin, cos = small_sincos(half * slab[cb, rt * SUB : rt * SUB + SUB] - shift)
                    fr = cos * turn_re + sin * turn_im
                    fi = cos * turn_im - sin * turn_re
                    for s in range(2):
                        re = src[2 * f + s, 0, cb + 2, rows(rt)]
                        im = src[2 * f + s, 1, cb + 2, rows(rt)]
                        dst[2 * f + s, 0, cb + 2, rows(rt)] = re * fr - im * fi
                        dst[2 * f + s, 1, cb + 2, rows(rt)] = re * fi + im * fr

    def rows_then_columns(src, dst):
        @pl.loop(0, fl * 2)
        def _(field):
            f = lax.div(field, 2)
            c0 = coefficients(f, 0)
            c1 = coefficients(f, 1)
            for rt in range(nrt):
                down = []
                for cb in range(nb):
                    x = [src[field, p, cb + 2, rows(rt)] for p in range(2)]
                    one = [src[field, p, cb + 2, rows(rt, 1)] + src[field, p, cb + 2, rows(rt, -1)] for p in range(2)]
                    two = [src[field, p, cb + 2, rows(rt, 2)] + src[field, p, cb + 2, rows(rt, -2)] for p in range(2)]
                    down.append(combine(c0, x, one, two))
                w = [around(down, p) for p in range(2)]
                put(
                    dst, field, rt,
                    [
                        combine(
                            c1,
                            down[cb],
                            [w[p][cb + 1] + w[p][cb - 1] for p in range(2)],
                            [w[p][cb + 2] + w[p][cb - 2] for p in range(2)],
                        )
                        for cb in range(nb)
                    ],
                )

    def slanted(src, field, c, rt, cb, way, rows=rows):
        x = [src[field, p, cb + 2, rows(rt)] for p in range(2)]
        one, two = (
            [
                src[field, p, cb + 2 + k * way, rows(rt, k)] + src[field, p, cb + 2 - k * way, rows(rt, -k)]
                for p in range(2)
            ]
            for k in (1, 2)
        )
        return combine(c, x, one, two)

    def first_slant(src, dst):
        @pl.loop(0, fl * 2)
        def _(field):
            c = coefficients(lax.div(field, 2), 2)
            for rt in range(nrt):
                put(dst, field, rt, [slanted(src, field, c, rt, cb, 1) for cb in range(nb)])

    def rows_at(rt, k=0):
        return pl.ds(pl.multiple_of(TOP + rt * SUB, SUB) + k, SUB)

    def second_slant(src, dst, part, keep, half):
        @pl.loop(0, nrt // 2)
        def _(k):
            rt = half * (nrt // 2) + k
            for f in range(fl):
                c = coefficients(f, 3)
                for cb in range(nb):
                    sr, si = slanted(src, 2 * f, c, rt, cb, -1, rows_at)
                    rr, ri = slanted(src, 2 * f + 1, c, rt, cb, -1, rows_at)
                    if keep:
                        dst[2 * f, 0, cb + 2, rows_at(rt)] = sr
                        dst[2 * f, 1, cb + 2, rows_at(rt)] = si
                        dst[2 * f + 1, 0, cb + 2, rows_at(rt)] = rr
                        dst[2 * f + 1, 1, cb + 2, rows_at(rt)] = ri
                    term = sr * rr - si * ri
                    if f > 0:
                        term = tile_load(part, nb, rt, cb) + term
                    tile_store(part, nb, rt, cb, term)

    c_copies = []
    nears = []

    def reduce_chip(t):
        nears[t].wait_recv()
        parts[t, own_half] = parts[t, own_half] + near[t]
        begin(c_copies[t])
        red[t, chip] = parts[t, mine]

    for t in range(steps):
        nears.append(remote(parts.at[t, other_half], near.at[t], near_send.at[t], near_recv.at[t], mate))
        c_copies.append(
            [
                remote(parts.at[t, place(partners[i])], red.at[t, chip], c_send.at[t, i], c_recv.at[t, i], partners[i])
                for i in alike
            ]
        )
    for t in range(steps):
        passes[t].wait_recv()
        lens(slabs.at[t], fx, fy)
        if t + 1 < steps:
            hand_on(t + 1)
        rows_then_columns(fy, fx)
        if t > 0:
            reduce_chip(t - 1)
        first_slant(fx, fy)
        second_slant(fy, fx, parts.at[t], t < steps - 1, 1 - side)
        nears[t].start()
        second_slant(fy, fx, parts.at[t], t < steps - 1, side)
    reduce_chip(steps - 1)

    sums = []
    for t in range(steps):
        for copy in c_copies[t]:
            copy.wait_recv()
        total = red[t, 0]
        for i in range(1, chips):
            total = total + red[t, i]
        sums.append(total / math.sqrt(freq_total))
    d_copies = []
    for i in list(rounds) + [0]:
        k = partners[i]
        value = sums[0] * (owner[0] == k).astype(jnp.float32)
        for t in range(1, steps):
            value = value + sums[t] * (owner[t] == k).astype(jnp.float32)
        if i == 0:
            out[mine] = value
        else:
            image[k] = value
            d_copies.append(remote(image.at[k], out.at[mine], d_send.at[i], d_recv.at[i], k))
            d_copies[-1].start()
    for copy in d_copies:
        copy.wait_recv()
    left(a_copies + b_copies[-1] + passes + nears + sum(c_copies, []) + d_copies)


def restore(got, out):
    nb = out.shape[2] // LANE
    for rt in range(out.shape[1] // SUB):
        tiles = butterfly([tile_load(got, nb, rt, cb) for cb in range(nb)])
        for v in range(nb):
            out[0, rt * SUB : rt * SUB + SUB, v * LANE : v * LANE + LANE] = tiles[v]


def local(n, receiver_data, source_spectrum, filter_taps, slowness, depth_owner, source_position):
    fl, _, height, breadth = receiver_data.shape
    steps = depth_owner.shape[0]
    nb = breadth // LANE
    nrt = height // SUB
    cr = height * nb // n
    slab = slowness[0].reshape(nrt, SUB, nb, LANE).transpose(0, 2, 1, 3).reshape(n, cr, LANE)
    chunks = (n, cr, LANE)
    vmem = pl.BlockSpec(memory_space=pltpu.VMEM)
    hbm = pl.BlockSpec(memory_space=pltpu.HBM)
    fields = (2 * fl, 2, nb + 4, height + 2 * TOP, LANE)
    dma = pltpu.SemaphoreType.DMA
    result = pl.pallas_call(
        functools.partial(kernel, n),
        out_shape=jax.ShapeDtypeStruct(chunks, jnp.float32),
        in_specs=[hbm] * 6,
        out_specs=vmem,
        scratch_shapes=[
            pltpu.SMEM(depth_owner.shape, jnp.int32),
            pltpu.SMEM(source_position.shape, jnp.int32),
            pltpu.SMEM(source_spectrum.shape, jnp.float32),
            pltpu.SMEM(filter_taps.shape, jnp.float32),
            dma((4,)),
            pltpu.VMEM(receiver_data.shape, jnp.float32),
            pltpu.VMEM(fields, jnp.float32),
            pltpu.VMEM(fields, jnp.float32),
            pltpu.VMEM((fl, 4, 5, SUB, LANE), jnp.float32),
            pltpu.VMEM((fl, 4, SUB, LANE), jnp.float32),
            pltpu.VMEM((nb, height, LANE), jnp.float32),
            pltpu.VMEM(chunks, jnp.float32),
            pltpu.VMEM((steps,) + chunks, jnp.float32),
            pltpu.VMEM((steps,) + chunks, jnp.float32),
            pltpu.VMEM((steps, n // 2, cr, LANE), jnp.float32),
            pltpu.VMEM((steps, n // 2, cr, LANE), jnp.float32),
            pltpu.VMEM(chunks, jnp.float32),
            dma,
            dma,
            dma((n,)),
            dma((n,)),
            dma((steps, n)),
            dma((steps, n)),
            dma((steps,)),
            dma((steps,)),
            dma((steps,)),
            dma((steps,)),
            dma((steps, n)),
            dma((steps, n)),
            dma((n,)),
            dma((n,)),
        ],
        compiler_params=pltpu.CompilerParams(
            collective_id=0, has_side_effects=True, vmem_limit_bytes=60 * 1024 * 1024
        ),
        name="migrate",
    )(depth_owner, source_position, source_spectrum, filter_taps, receiver_data, slab)
    return pl.pallas_call(
        restore,
        out_shape=jax.ShapeDtypeStruct((1, height, breadth), jnp.float32),
        in_specs=[vmem],
        out_specs=vmem,
        name="restore",
    )(result)


def solution(mesh):
    return jax.shard_map(
        functools.partial(local, mesh.shape["freq"]),
        mesh=mesh,
        in_specs=(
            P(("shot", "freq"), None, None, None),
            P("freq", None),
            P("freq", None, None),
            P("freq", None, None),
            P("shot"),
            P("shot"),
        ),
        out_specs=P(("shot", "freq"), None, None),
        check_vma=False,
    )
```

```python
import functools
import math

import jax
import jax.numpy as jnp
from jax import lax
from jax.experimental import pallas as pl
from jax.experimental.pallas import tpu as pltpu
from jax.sharding import PartitionSpec as P

lens_rate = 3.0
wave_rate = 0.5
middle = 1.25
MESH = pl.DeviceIdType.MESH
SUB = 8
LANE = 128
TOP = 8


def sincos(x):
    k = jnp.floor(x * (2.0 / math.pi) + 0.5)
    r = x - k * 1.5703125
    r = r - k * 4.837512969970703125e-4
    r = r - k * 7.54978995489188216e-8
    q = k.astype(jnp.int32)
    z = r * r
    s = r + r * z * (-1.6666654611e-1 + z * (8.3321608736e-3 - z * 1.9515295891e-4))
    c = 1.0 - 0.5 * z + z * z * (
        4.166664568298827e-2 + z * (-1.388731625493765e-3 + z * 2.443315711809948e-5)
    )
    swap = (q & 1) == 1
    sin = jnp.where(swap, c, s)
    cos = jnp.where(swap, s, c)
    sin = jnp.where((q & 2) == 2, -sin, sin)
    cos = jnp.where(((q + 1) & 2) == 2, -cos, cos)
    return sin, cos


def small_sincos(h):
    z = h * h
    s = h * (1.4142132220 + z * (-0.23569866110 + z * (0.011774833848 + z * -2.6969778329e-4)))
    c = 1.4142135600 + z * (-0.70710668609 + z * (0.058924962733 + z * (-1.9628489073e-3 + z * 3.3861135969e-5)))
    return s * c, 1.0 - s * s


def lane_index():
    return lax.broadcasted_iota(jnp.int32, (SUB, LANE), 1)


def exchanges(nb):
    bits = nb.bit_length() - 1
    pairs, held = [], []
    for k in range(bits):
        at = LANE.bit_length() - 1 + k
        while at >= bits:
            at -= bits
            pairs.append((k, at))
        held.append(at)
    order = [sum((cb >> held[k] & 1) << k for k in range(bits)) for cb in range(nb)]
    return pairs, order


def exchange(tiles, pairs):
    lanes = lane_index()
    tiles = list(tiles)
    for k, at in pairs:
        step = 1 << at
        low = (lanes & step) == 0
        for v in range(len(tiles)):
            if v >> k & 1 == 0:
                w = v + (1 << k)
                a, b = tiles[v], tiles[w]
                tiles[v] = jnp.where(low, a, pltpu.roll(b, step, 1))
                tiles[w] = jnp.where(low, pltpu.roll(a, LANE - step, 1), b)
    return tiles


def interleave(tiles):
    pairs, order = exchanges(len(tiles))
    moved = exchange(tiles, pairs)
    return [moved[v] for v in order]


def deinterleave(tiles):
    pairs, order = exchanges(len(tiles))
    moved = [None] * len(tiles)
    for cb, v in enumerate(order):
        moved[v] = tiles[cb]
    return exchange(moved, pairs[::-1])


def pieces(cr, nb, rt, cb):
    row = cb * SUB
    size = min(cr, SUB)
    return [(rt * (nb * SUB // cr) + (row + o) // cr, (row + o) % cr, size, o) for o in range(0, SUB, size)]


def tile_load(ref, nb, rt, cb):
    got = [ref[c, r : r + m] for c, r, m, _ in pieces(ref.shape[1], nb, rt, cb)]
    return got[0] if len(got) == 1 else jnp.concatenate(got, axis=0)


def tile_store(ref, nb, rt, cb, value):
    for c, r, m, o in pieces(ref.shape[1], nb, rt, cb):
        ref[c, r : r + m] = value[o : o + m]


def kernel(
    n,
    owner_hbm,
    position_hbm,
    spectrum_hbm,
    taps_hbm,
    recv_hbm,
    slow,
    out,
    owner,
    position,
    spectrum,
    taps,
    small_sem,
    rbuf,
    fx,
    fy,
    coefs,
    turns,
    own_slow,
    own_tiles,
    all_slow,
    slabs,
    parts,
    near,
    red,
    image,
    load_sem,
    own_sem,
    a_send,
    a_recv,
    b_send,
    b_recv,
    pass_send,
    pass_recv,
    near_send,
    near_recv,
    c_send,
    c_recv,
    d_send,
    d_recv,
):
    me = lax.axis_index("freq")
    steps = owner.shape[0]
    fl = rbuf.shape[0]
    height = rbuf.shape[2]
    breadth = rbuf.shape[3]
    nb = breadth // LANE
    nrt = height // SUB
    freq_total = n * fl
    first = me * fl

    def peer(i):
        if n & (n - 1):
            return lax.rem(me + i, n)
        to = 0
        for b in range(n.bit_length() - 1):
            bit = lax.rem(lax.div(me, 1 << b), 2)
            to = to + (1 << b) * (1 - bit if i >> b & 1 else bit)
        return to

    partners = [peer(i) for i in range(n)]
    rounds = range(n - 1, 0, -1)
    alike = range(n - 2, 0, -2)
    chips = n // 2
    side = lax.rem(me, 2)
    chip = lax.div(me, 2)
    mate = partners[1]

    def place(device):
        return lax.rem(device, 2) * chips + lax.div(device, 2)

    mine = place(me)
    own_half = pl.ds(side * chips, chips)
    other_half = pl.ds((1 - side) * chips, chips)

    def remote(src, dst, send, recv, to):
        return pltpu.make_async_remote_copy(
            src_ref=src, dst_ref=dst, send_sem=send, recv_sem=recv,
            device_id={"freq": to}, device_id_type=MESH,
        )

    own = pltpu.make_async_copy(slow, own_slow, own_sem)
    own.start()
    barrier = pltpu.get_barrier_semaphore()
    for i in rounds:
        pl.semaphore_signal(barrier, inc=1, device_id={"freq": partners[i]}, device_id_type=MESH)
    load = pltpu.make_async_copy(recv_hbm, rbuf, load_sem)
    load.start()
    small = [
        pltpu.make_async_copy(src, dst, small_sem.at[j])
        for j, (src, dst) in enumerate(
            ((owner_hbm, owner), (position_hbm, position), (spectrum_hbm, spectrum), (taps_hbm, taps))
        )
    ]
    for copy in small:
        copy.start()
    own.wait()
    for rt in range(nrt):
        tiles = interleave([tile_load(own_slow, nb, rt, v) for v in range(nb)])
        for cb in range(nb):
            tile_store(own_tiles, nb, rt, cb, tiles[cb])
    pl.semaphore_wait(barrier, n - 1)

    a_copies = [
        remote(own_tiles.at[place(partners[i])], all_slow.at[me], a_send.at[i], a_recv.at[i], partners[i])
        for i in rounds
    ]
    for copy in a_copies:
        copy.start()
    all_slow[me] = own_tiles[mine]

    def rows(rt, k=0):
        start = TOP + rt * SUB + k
        return slice(start, start + SUB)

    lanes = lane_index()
    zero = jnp.zeros((SUB, LANE), jnp.float32)

    @pl.loop(0, fl * 2)
    def _(field):
        for part in range(2):
            for cx in range(nb + 4):
                for buf in (fx, fy):
                    buf[field, part, cx, 0:TOP] = zero
                    buf[field, part, cx, TOP + height : 2 * TOP + height] = zero

    for copy in small:
        copy.wait()

    @pl.loop(0, fl)
    def _(f):
        half = jnp.broadcast_to(((first + f).astype(jnp.float32) + 1.0) * (lens_rate / freq_total * 0.5), (SUB, LANE))
        sin, cos = sincos(half * (2.0 * middle))
        turn_re, turn_im = cos, -sin
        for d in range(4):
            c = [jnp.broadcast_to(taps[f, d, j], (SUB, LANE)) for j in range(6)]
            m = jnp.maximum(jnp.abs(c[0]), jnp.abs(c[1]))
            some = m > 0.0
            inverse = 1.0 / jnp.where(some, m, 1.0)
            ur = jnp.where(some, c[0] * inverse, 1.0)
            ui = jnp.where(some, c[1] * inverse, 0.0)
            q = ur * ur + ui * ui
            root = 1.0 / jnp.sqrt(q)
            root = root * (1.5 - 0.5 * q * root * root)
            pr = ur * root
            pi = ui * root
            turn_re, turn_im = turn_re * pr - turn_im * pi, turn_re * pi + turn_im * pr
            coefs[f, d, 0] = m * (q * root)
            for j in (1, 3):
                coefs[f, d, j] = c[j + 1] * pr + c[j + 2] * pi
                coefs[f, d, j + 1] = c[j + 2] * pr - c[j + 1] * pi
        turns[f, 0] = half
        turns[f, 1] = half * middle
        turns[f, 2] = turn_re
        turns[f, 3] = turn_im

    src_row = position[0].astype(jnp.float32)
    src_col = position[1].astype(jnp.float32)
    subs = lax.broadcasted_iota(jnp.int32, (SUB, LANE), 0)
    across = lanes * nb

    @pl.loop(0, nrt)
    def _(rt):
        row = (subs + rt * SUB).astype(jnp.float32) - src_row
        at = pl.ds(pl.multiple_of(TOP + rt * SUB, SUB), SUB)
        for cb in range(nb):
            col = (across + cb).astype(jnp.float32) - src_col
            distance = jnp.sqrt(row * row + col * col + 1.0)
            amplitude = 1.0 / (1.0 + distance / (height / 4.0))
            for f in range(fl):
                number = ((first + f).astype(jnp.float32) + 1.0) * (wave_rate / freq_total)
                sin, cos = sincos(number * distance)
                base_re = amplitude * cos
                base_im = -amplitude * sin
                wr = spectrum[f, 0]
                wi = spectrum[f, 1]
                fx[2 * f, 0, cb + 2, at] = wr * base_re - wi * base_im
                fx[2 * f, 1, cb + 2, at] = wr * base_im + wi * base_re

    load.wait()

    @pl.loop(0, fl)
    def _(f):
        for part in range(2):
            for rt in range(nrt):
                tiles = interleave(
                    [rbuf[f, part, rt * SUB : rt * SUB + SUB, v * LANE : v * LANE + LANE] for v in range(nb)]
                )
                for cb in range(nb):
                    fx[2 * f + 1, part, cb + 2, rows(rt)] = tiles[cb] if part == 0 else -tiles[cb]

    def arrived(copies):
        for copy in reversed(copies):
            copy.wait_recv()

    arrived(a_copies)
    b_copies = []
    passes = []
    for t in range(steps):
        slabs[t, mine] = all_slow[owner[t]]
        b_copies.append(
            [
                remote(slabs.at[t, mine], slabs.at[t, mine], b_send.at[t, i], b_recv.at[t, i], partners[i])
                for i in alike
            ]
        )
        passes.append(remote(slabs.at[t, own_half], slabs.at[t, own_half], pass_send.at[t], pass_recv.at[t], mate))

    def begin(copies):
        for copy in copies:
            copy.start()

    def left(copies):
        for copy in copies:
            copy.wait_send()

    def hand_on(t):
        arrived(b_copies[t])
        passes[t].start()

    begin(b_copies[0])
    for t in range(1, steps):
        left(b_copies[t - 1])
        begin(b_copies[t])
    hand_on(0)

    def after(x):
        return jnp.where(lanes == LANE - 1, 0.0, pltpu.roll(x, LANE - 1, 1))

    def before(x):
        return jnp.where(lanes == 0, 0.0, pltpu.roll(x, 1, 1))

    edges_first = [0, 1, nb - 2, nb - 1] + list(range(2, nb - 2))

    def combine(c, x, one, two):
        (xr, xi), (pr, pi), (qr, qi) = x, one, two
        re = c[0] * xr + (c[1] * pr - c[2] * pi) + (c[3] * qr - c[4] * qi)
        im = c[0] * xi + (c[1] * pi + c[2] * pr) + (c[3] * qi + c[4] * qr)
        return re, im

    def coefficients(f, d):
        return [coefs[f, d, j] for j in range(5)]

    def around(got, p):
        whole = {cb: got[cb][p] for cb in range(nb)}
        for k in range(2):
            whole[nb + k] = after(got[k][p])
            whole[k - 2] = before(got[nb - 2 + k][p])
        return whole

    def put(dst, field, rt, got):
        for p in range(2):
            whole = around(got, p)
            for cb in range(-2, nb + 2):
                dst[field, p, cb + 2, rows(rt)] = whole[cb]

    def lens(slow_now, src, dst):
        @pl.loop(0, fl)
        def _(f):
            half, shift, turn_re, turn_im = (turns[f, j] for j in range(4))
            for rt in range(nrt):
                for cb in range(nb):
                    sin, cos = small_sincos(half * tile_load(slow_now, nb, rt, cb) - shift)
                    fr = cos * turn_re + sin * turn_im
                    fi = cos * turn_im - sin * turn_re
                    for s in range(2):
                        re = src[2 * f + s, 0, cb + 2, rows(rt)]
                        im = src[2 * f + s, 1, cb + 2, rows(rt)]
                        dst[2 * f + s, 0, cb + 2, rows(rt)] = re * fr - im * fi
                        dst[2 * f + s, 1, cb + 2, rows(rt)] = re * fi + im * fr

    def rows_then_columns(src, dst):
        @pl.loop(0, fl * 2)
        def _(field):
            f = lax.div(field, 2)
            c0 = coefficients(f, 0)
            c1 = coefficients(f, 1)
            for rt in range(nrt):
                down = {}
                for cb in edges_first:
                    x = [src[field, p, cb + 2, rows(rt)] for p in range(2)]
                    one = [src[field, p, cb + 2, rows(rt, 1)] + src[field, p, cb + 2, rows(rt, -1)] for p in range(2)]
                    two = [src[field, p, cb + 2, rows(rt, 2)] + src[field, p, cb + 2, rows(rt, -2)] for p in range(2)]
                    down[cb] = combine(c0, x, one, two)
                w = [around(down, p) for p in range(2)]
                put(
                    dst, field, rt,
                    {
                        cb: combine(
                            c1,
                            down[cb],
                            [w[p][cb + 1] + w[p][cb - 1] for p in range(2)],
                            [w[p][cb + 2] + w[p][cb - 2] for p in range(2)],
                        )
                        for cb in edges_first
                    },
                )

    def slanted(src, field, c, rt, cb, way, rows=rows):
        x = [src[field, p, cb + 2, rows(rt)] for p in range(2)]
        one, two = (
            [
                src[field, p, cb + 2 + k * way, rows(rt, k)] + src[field, p, cb + 2 - k * way, rows(rt, -k)]
                for p in range(2)
            ]
            for k in (1, 2)
        )
        return combine(c, x, one, two)

    def first_slant(src, dst):
        @pl.loop(0, fl * 2)
        def _(field):
            c = coefficients(lax.div(field, 2), 2)
            for rt in range(nrt):
                put(dst, field, rt, {cb: slanted(src, field, c, rt, cb, 1) for cb in edges_first})

    def rows_at(rt, k=0):
        return pl.ds(pl.multiple_of(TOP + rt * SUB, SUB) + k, SUB)

    def second_slant(src, dst, part, keep, half):
        @pl.loop(0, nrt // 2)
        def _(k):
            rt = half * (nrt // 2) + k
            for f in range(fl):
                c = coefficients(f, 3)
                for cb in range(nb):
                    sr, si = slanted(src, 2 * f, c, rt, cb, -1, rows_at)
                    rr, ri = slanted(src, 2 * f + 1, c, rt, cb, -1, rows_at)
                    if keep:
                        dst[2 * f, 0, cb + 2, rows_at(rt)] = sr
                        dst[2 * f, 1, cb + 2, rows_at(rt)] = si
                        dst[2 * f + 1, 0, cb + 2, rows_at(rt)] = rr
                        dst[2 * f + 1, 1, cb + 2, rows_at(rt)] = ri
                    term = sr * rr - si * ri
                    if f > 0:
                        term = tile_load(part, nb, rt, cb) + term
                    tile_store(part, nb, rt, cb, term)

    c_copies = []
    nears = []

    def reduce_chip(t):
        nears[t].wait_recv()
        parts[t, own_half] = parts[t, own_half] + near[t]
        begin(c_copies[t])
        red[t, chip] = parts[t, mine]

    for t in range(steps):
        nears.append(remote(parts.at[t, other_half], near.at[t], near_send.at[t], near_recv.at[t], mate))
        c_copies.append(
            [
                remote(parts.at[t, place(partners[i])], red.at[t, chip], c_send.at[t, i], c_recv.at[t, i], partners[i])
                for i in alike
            ]
        )
    for t in range(steps):
        passes[t].wait_recv()
        lens(slabs.at[t], fx, fy)
        rows_then_columns(fy, fx)
        if t + 1 < steps:
            hand_on(t + 1)
        if t > 0:
            reduce_chip(t - 1)
        first_slant(fx, fy)
        second_slant(fy, fx, parts.at[t], t < steps - 1, 1 - side)
        nears[t].start()
        second_slant(fy, fx, parts.at[t], t < steps - 1, side)
    reduce_chip(steps - 1)

    sums = []
    for t in range(steps):
        arrived(c_copies[t])
        total = red[t, 0]
        for i in range(1, chips):
            total = total + red[t, i]
        sums.append(total / math.sqrt(freq_total))
    d_copies = []
    for i in list(rounds) + [0]:
        k = partners[i]
        value = sums[0] * (owner[0] == k).astype(jnp.float32)
        for t in range(1, steps):
            value = value + sums[t] * (owner[t] == k).astype(jnp.float32)
        if i == 0:
            out[mine] = value
        else:
            image[k] = value
            d_copies.append(remote(image.at[k], out.at[mine], d_send.at[i], d_recv.at[i], k))
            d_copies[-1].start()
    left(a_copies + b_copies[-1] + passes + nears + sum(c_copies, []) + d_copies)
    arrived(d_copies)


def restore(got, out):
    nb = out.shape[2] // LANE
    for rt in range(out.shape[1] // SUB):
        tiles = deinterleave([tile_load(got, nb, rt, cb) for cb in range(nb)])
        for v in range(nb):
            out[0, rt * SUB : rt * SUB + SUB, v * LANE : v * LANE + LANE] = tiles[v]


def local(n, receiver_data, source_spectrum, filter_taps, slowness, depth_owner, source_position):
    fl, _, height, breadth = receiver_data.shape
    steps = depth_owner.shape[0]
    nb = breadth // LANE
    nrt = height // SUB
    cr = height * nb // n
    slab = slowness[0].reshape(nrt, SUB, nb, LANE).transpose(0, 2, 1, 3).reshape(n, cr, LANE)
    chunks = (n, cr, LANE)
    vmem = pl.BlockSpec(memory_space=pltpu.VMEM)
    hbm = pl.BlockSpec(memory_space=pltpu.HBM)
    fields = (2 * fl, 2, nb + 4, height + 2 * TOP, LANE)
    dma = pltpu.SemaphoreType.DMA
    result = pl.pallas_call(
        functools.partial(kernel, n),
        out_shape=pltpu.VMEM(chunks, jnp.float32),
        in_specs=[hbm] * 6,
        out_specs=vmem,
        scratch_shapes=[
            pltpu.SMEM(depth_owner.shape, jnp.int32),
            pltpu.SMEM(source_position.shape, jnp.int32),
            pltpu.SMEM(source_spectrum.shape, jnp.float32),
            pltpu.SMEM(filter_taps.shape, jnp.float32),
            dma((4,)),
            pltpu.VMEM(receiver_data.shape, jnp.float32),
            pltpu.VMEM(fields, jnp.float32),
            pltpu.VMEM(fields, jnp.float32),
            pltpu.VMEM((fl, 4, 5, SUB, LANE), jnp.float32),
            pltpu.VMEM((fl, 4, SUB, LANE), jnp.float32),
            pltpu.VMEM(chunks, jnp.float32),
            pltpu.VMEM(chunks, jnp.float32),
            pltpu.VMEM(chunks, jnp.float32),
            pltpu.VMEM((steps,) + chunks, jnp.float32),
            pltpu.VMEM((steps,) + chunks, jnp.float32),
            pltpu.VMEM((steps, n // 2, cr, LANE), jnp.float32),
            pltpu.VMEM((steps, n // 2, cr, LANE), jnp.float32),
            pltpu.VMEM(chunks, jnp.float32),
            dma,
            dma,
            dma((n,)),
            dma((n,)),
            dma((steps, n)),
            dma((steps, n)),
            dma((steps,)),
            dma((steps,)),
            dma((steps,)),
            dma((steps,)),
            dma((steps, n)),
            dma((steps, n)),
            dma((n,)),
            dma((n,)),
        ],
        compiler_params=pltpu.CompilerParams(
            collective_id=0, has_side_effects=True, vmem_limit_bytes=40 * 1024 * 1024
        ),
        name="migrate",
    )(*[pltpu.with_memory_space_constraint(x, pltpu.HBM) for x in (depth_owner, source_position, source_spectrum, filter_taps, receiver_data, slab)])
    return pl.pallas_call(
        restore,
        out_shape=jax.ShapeDtypeStruct((1, height, breadth), jnp.float32),
        in_specs=[vmem],
        out_specs=vmem,
        name="restore",
    )(pltpu.with_memory_space_constraint(result, pltpu.VMEM))


def solution(mesh):
    return jax.shard_map(
        functools.partial(local, mesh.shape["freq"]),
        mesh=mesh,
        in_specs=(
            P(("shot", "freq"), None, None, None),
            P("freq", None),
            P("freq", None, None),
            P("freq", None, None),
            P("shot"),
            P("shot"),
        ),
        out_specs=P(("shot", "freq"), None, None),
        check_vma=False,
    )
```

```python
import functools
import math

import jax
import jax.numpy as jnp
from jax import lax
from jax.experimental import pallas as pl
from jax.experimental.pallas import tpu as pltpu
from jax.sharding import PartitionSpec as P

lens_rate = 3.0
wave_rate = 0.5
middle = 1.25
MESH = pl.DeviceIdType.MESH
SUB = 8
LANE = 128
TOP = 8


def sincos(x):
    k = jnp.floor(x * (2.0 / math.pi) + 0.5)
    r = x - k * 1.5703125
    r = r - k * 4.837512969970703125e-4
    r = r - k * 7.54978995489188216e-8
    q = k.astype(jnp.int32)
    z = r * r
    s = r + r * z * (-1.6666654611e-1 + z * (8.3321608736e-3 - z * 1.9515295891e-4))
    c = 1.0 - 0.5 * z + z * z * (
        4.166664568298827e-2 + z * (-1.388731625493765e-3 + z * 2.443315711809948e-5)
    )
    swap = (q & 1) == 1
    sin = jnp.where(swap, c, s)
    cos = jnp.where(swap, s, c)
    sin = jnp.where((q & 2) == 2, -sin, sin)
    cos = jnp.where(((q + 1) & 2) == 2, -cos, cos)
    return sin, cos


def small_sincos(h):
    z = h * h
    s = h * (1.4142132220 + z * (-0.23569866110 + z * (0.011774833848 + z * -2.6969778329e-4)))
    c = 1.4142135600 + z * (-0.70710668609 + z * (0.058924962733 + z * (-1.9628489073e-3 + z * 3.3861135969e-5)))
    return s * c, 1.0 - s * s


def lane_index():
    return lax.broadcasted_iota(jnp.int32, (SUB, LANE), 1)


def exchanges(nb):
    bits = nb.bit_length() - 1
    pairs, held = [], []
    for k in range(bits):
        at = LANE.bit_length() - 1 + k
        while at >= bits:
            at -= bits
            pairs.append((k, at))
        held.append(at)
    order = [sum((cb >> held[k] & 1) << k for k in range(bits)) for cb in range(nb)]
    return pairs, order


def exchange(tiles, pairs):
    lanes = lane_index()
    tiles = list(tiles)
    for k, at in pairs:
        step = 1 << at
        low = (lanes & step) == 0
        for v in range(len(tiles)):
            if v >> k & 1 == 0:
                w = v + (1 << k)
                a, b = tiles[v], tiles[w]
                tiles[v] = jnp.where(low, a, pltpu.roll(b, step, 1))
                tiles[w] = jnp.where(low, pltpu.roll(a, LANE - step, 1), b)
    return tiles


def interleave(tiles):
    pairs, order = exchanges(len(tiles))
    moved = exchange(tiles, pairs)
    return [moved[v] for v in order]


def deinterleave(tiles):
    pairs, order = exchanges(len(tiles))
    moved = [None] * len(tiles)
    for cb, v in enumerate(order):
        moved[v] = tiles[cb]
    return exchange(moved, pairs[::-1])


def pieces(cr, nb, rt, cb):
    row = cb * SUB
    size = min(cr, SUB)
    return [(rt * (nb * SUB // cr) + (row + o) // cr, (row + o) % cr, size, o) for o in range(0, SUB, size)]


def tile_load(ref, nb, rt, cb):
    got = [ref[c, r : r + m] for c, r, m, _ in pieces(ref.shape[1], nb, rt, cb)]
    return got[0] if len(got) == 1 else jnp.concatenate(got, axis=0)


def tile_store(ref, nb, rt, cb, value):
    for c, r, m, o in pieces(ref.shape[1], nb, rt, cb):
        ref[c, r : r + m] = value[o : o + m]


def kernel(
    n,
    owner_hbm,
    position_hbm,
    spectrum_hbm,
    taps_hbm,
    recv_hbm,
    slow,
    out,
    owner,
    position,
    spectrum,
    taps,
    small_sem,
    rbuf,
    fx,
    fy,
    coefs,
    turns,
    own_slow,
    own_tiles,
    all_slow,
    slabs,
    parts,
    near,
    red,
    image,
    load_sem,
    own_sem,
    a_send,
    a_recv,
    b_send,
    b_recv,
    pass_send,
    pass_recv,
    near_send,
    near_recv,
    c_send,
    c_recv,
    d_send,
    d_recv,
):
    me = lax.axis_index("freq")
    steps = owner.shape[0]
    fl = rbuf.shape[0]
    height = rbuf.shape[2]
    breadth = rbuf.shape[3]
    nb = breadth // LANE
    nrt = height // SUB
    freq_total = n * fl
    first = me * fl

    def peer(i):
        if n & (n - 1):
            return lax.rem(me + i, n)
        to = 0
        for b in range(n.bit_length() - 1):
            bit = lax.rem(lax.div(me, 1 << b), 2)
            to = to + (1 << b) * (1 - bit if i >> b & 1 else bit)
        return to

    partners = [peer(i) for i in range(n)]
    rounds = range(n - 1, 0, -1)
    alike = range(n - 2, 0, -2)
    chips = n // 2
    side = lax.rem(me, 2)
    chip = lax.div(me, 2)
    mate = partners[1]

    def place(device):
        return lax.rem(device, 2) * chips + lax.div(device, 2)

    mine = place(me)
    own_half = pl.ds(side * chips, chips)
    other_half = pl.ds((1 - side) * chips, chips)

    def remote(src, dst, send, recv, to):
        return pltpu.make_async_remote_copy(
            src_ref=src, dst_ref=dst, send_sem=send, recv_sem=recv,
            device_id={"freq": to}, device_id_type=MESH,
        )

    own = pltpu.make_async_copy(slow, own_slow, own_sem)
    own.start()
    barrier = pltpu.get_barrier_semaphore()
    for i in rounds:
        pl.semaphore_signal(barrier, inc=1, device_id={"freq": partners[i]}, device_id_type=MESH)
    load = pltpu.make_async_copy(recv_hbm, rbuf, load_sem)
    load.start()
    small = [
        pltpu.make_async_copy(src, dst, small_sem.at[j])
        for j, (src, dst) in enumerate(
            ((owner_hbm, owner), (position_hbm, position), (spectrum_hbm, spectrum), (taps_hbm, taps))
        )
    ]
    for copy in small:
        copy.start()
    own.wait()
    for rt in range(nrt):
        tiles = interleave([tile_load(own_slow, nb, rt, v) for v in range(nb)])
        for cb in range(nb):
            tile_store(own_tiles, nb, rt, cb, tiles[cb])
    pl.semaphore_wait(barrier, n - 1)

    a_copies = [
        remote(own_tiles.at[place(partners[i])], all_slow.at[me], a_send, a_recv, partners[i])
        for i in rounds
    ]
    for copy in a_copies:
        copy.start()
    all_slow[me] = own_tiles[mine]

    def rows(rt, k=0):
        start = TOP + rt * SUB + k
        return slice(start, start + SUB)

    lanes = lane_index()
    zero = jnp.zeros((SUB, LANE), jnp.float32)

    @pl.loop(0, fl * 2)
    def _(field):
        for part in range(2):
            for cx in range(nb + 4):
                for buf in (fx, fy):
                    buf[field, part, cx, 0:TOP] = zero
                    buf[field, part, cx, TOP + height : 2 * TOP + height] = zero
                    if cx < 2 or cx >= nb + 2:
                        for rt in range(nrt):
                            buf[field, part, cx, rows(rt)] = zero

    for copy in small:
        copy.wait()

    @pl.loop(0, fl)
    def _(f):
        half = jnp.broadcast_to(((first + f).astype(jnp.float32) + 1.0) * (lens_rate / freq_total * 0.5), (SUB, LANE))
        sin, cos = sincos(half * (2.0 * middle))
        turn_re, turn_im = cos, -sin
        for d in range(4):
            c = [jnp.broadcast_to(taps[f, d, j], (SUB, LANE)) for j in range(6)]
            m = jnp.maximum(jnp.abs(c[0]), jnp.abs(c[1]))
            some = m > 0.0
            inverse = 1.0 / jnp.where(some, m, 1.0)
            ur = jnp.where(some, c[0] * inverse, 1.0)
            ui = jnp.where(some, c[1] * inverse, 0.0)
            q = ur * ur + ui * ui
            root = 1.0 / jnp.sqrt(q)
            root = root * (1.5 - 0.5 * q * root * root)
            pr = ur * root
            pi = ui * root
            turn_re, turn_im = turn_re * pr - turn_im * pi, turn_re * pi + turn_im * pr
            coefs[f, d, 0] = m * (q * root)
            for j in (1, 3):
                coefs[f, d, j] = c[j + 1] * pr + c[j + 2] * pi
                coefs[f, d, j + 1] = c[j + 2] * pr - c[j + 1] * pi
        turns[f, 0] = half
        turns[f, 1] = half * middle
        turns[f, 2] = turn_re
        turns[f, 3] = turn_im

    src_row = position[0].astype(jnp.float32)
    src_col = position[1].astype(jnp.float32)
    subs = lax.broadcasted_iota(jnp.int32, (SUB, LANE), 0)
    across = lanes * nb

    @pl.loop(0, nrt)
    def _(rt):
        row = (subs + rt * SUB).astype(jnp.float32) - src_row
        at = pl.ds(pl.multiple_of(TOP + rt * SUB, SUB), SUB)
        for cb in range(nb):
            col = (across + cb).astype(jnp.float32) - src_col
            distance = jnp.sqrt(row * row + col * col + 1.0)
            amplitude = 1.0 / (1.0 + distance / (height / 4.0))
            for f in range(fl):
                number = ((first + f).astype(jnp.float32) + 1.0) * (wave_rate / freq_total)
                sin, cos = sincos(number * distance)
                base_re = amplitude * cos
                base_im = -amplitude * sin
                wr = spectrum[f, 0]
                wi = spectrum[f, 1]
                fx[2 * f, 0, cb + 2, at] = wr * base_re - wi * base_im
                fx[2 * f, 1, cb + 2, at] = wr * base_im + wi * base_re

    load.wait()

    @pl.loop(0, fl)
    def _(f):
        for part in range(2):
            for rt in range(nrt):
                tiles = interleave(
                    [rbuf[f, part, rt * SUB : rt * SUB + SUB, v * LANE : v * LANE + LANE] for v in range(nb)]
                )
                for cb in range(nb):
                    fx[2 * f + 1, part, cb + 2, rows(rt)] = tiles[cb] if part == 0 else -tiles[cb]

    def settle(count, sem):
        space = all_slow.at[0:count]
        pltpu.make_async_copy(space, space, sem).wait()

    settle(n - 1, a_recv)
    b_copies = []
    passes = []
    for t in range(steps):
        slabs[t, mine] = all_slow[owner[t]]
        b_copies.append(
            [
                remote(slabs.at[t, mine], slabs.at[t, mine], b_send.at[t], b_recv.at[t], partners[i])
                for i in alike
            ]
        )
        passes.append(remote(slabs.at[t, own_half], slabs.at[t, own_half], pass_send.at[t], pass_recv.at[t], mate))

    def begin(copies):
        for copy in copies:
            copy.start()

    def hand_on(t):
        settle(chips - 1, b_recv.at[t])
        passes[t].start()

    begin(b_copies[0])
    for t in range(1, steps):
        settle(chips - 1, b_send.at[t - 1])
        begin(b_copies[t])
    hand_on(0)

    def after(x):
        return jnp.where(lanes == LANE - 1, 0.0, pltpu.roll(x, LANE - 1, 1))

    def before(x):
        return jnp.where(lanes == 0, 0.0, pltpu.roll(x, 1, 1))

    edges_first = [0, 1, nb - 2, nb - 1] + list(range(2, nb - 2))

    def combine(c, x, one, two):
        (xr, xi), (pr, pi), (qr, qi) = x, one, two
        re = c[0] * xr + (c[1] * pr - c[2] * pi) + (c[3] * qr - c[4] * qi)
        im = c[0] * xi + (c[1] * pi + c[2] * pr) + (c[3] * qi + c[4] * qr)
        return re, im

    def coefficients(f, d):
        return [coefs[f, d, j] for j in range(5)]

    def around(got, p):
        whole = {cb: got[cb][p] for cb in range(nb)}
        for k in range(2):
            whole[nb + k] = after(got[k][p])
            whole[k - 2] = before(got[nb - 2 + k][p])
        return whole

    def put(dst, field, rt, got):
        for p in range(2):
            for cb in got:
                dst[field, p, cb + 2, rows(rt)] = got[cb][p]
            for k in range(2):
                pltpu.store(
                    dst.at[field, p, nb + 2 + k, rows(rt)], pltpu.roll(got[k][p], LANE - 1, 1), mask=lanes < LANE - 1
                )
                pltpu.store(dst.at[field, p, k, rows(rt)], pltpu.roll(got[nb - 2 + k][p], 1, 1), mask=lanes > 0)

    def lens(slow_now, src, dst):
        @pl.loop(0, fl)
        def _(f):
            half, shift, turn_re, turn_im = (turns[f, j] for j in range(4))
            for rt in range(nrt):
                for cb in range(nb):
                    sin, cos = small_sincos(half * tile_load(slow_now, nb, rt, cb) - shift)
                    fr = cos * turn_re + sin * turn_im
                    fi = cos * turn_im - sin * turn_re
                    for s in range(2):
                        re = src[2 * f + s, 0, cb + 2, rows(rt)]
                        im = src[2 * f + s, 1, cb + 2, rows(rt)]
                        dst[2 * f + s, 0, cb + 2, rows(rt)] = re * fr - im * fi
                        dst[2 * f + s, 1, cb + 2, rows(rt)] = re * fi + im * fr

    def rows_then_columns(src, dst):
        @pl.loop(0, fl)
        def _(f):
            c0 = coefficients(f, 0)
            c1 = coefficients(f, 1)
            for s in range(2):
                field = 2 * f + s
                for rt in range(nrt):
                    down = {}
                    for cb in edges_first:
                        x = [src[field, p, cb + 2, rows(rt)] for p in range(2)]
                        one = [src[field, p, cb + 2, rows(rt, 1)] + src[field, p, cb + 2, rows(rt, -1)] for p in range(2)]
                        two = [src[field, p, cb + 2, rows(rt, 2)] + src[field, p, cb + 2, rows(rt, -2)] for p in range(2)]
                        down[cb] = combine(c0, x, one, two)
                    w = [around(down, p) for p in range(2)]
                    put(
                        dst, field, rt,
                        {
                            cb: combine(
                                c1,
                                down[cb],
                                [w[p][cb + 1] + w[p][cb - 1] for p in range(2)],
                                [w[p][cb + 2] + w[p][cb - 2] for p in range(2)],
                            )
                            for cb in edges_first
                        },
                    )

    def slanted(src, field, c, rt, cb, way, rows=rows):
        x = [src[field, p, cb + 2, rows(rt)] for p in range(2)]
        one, two = (
            [
                src[field, p, cb + 2 + k * way, rows(rt, k)] + src[field, p, cb + 2 - k * way, rows(rt, -k)]
                for p in range(2)
            ]
            for k in (1, 2)
        )
        return combine(c, x, one, two)

    def first_slant(src, dst):
        @pl.loop(0, fl)
        def _(f):
            c = coefficients(f, 2)
            for s in range(2):
                for rt in range(nrt):
                    put(dst, 2 * f + s, rt, {cb: slanted(src, 2 * f + s, c, rt, cb, 1) for cb in edges_first})

    def rows_at(rt, k=0):
        return pl.ds(pl.multiple_of(TOP + rt * SUB, SUB) + k, SUB)

    def second_slant(src, dst, part, keep, half):
        @pl.loop(0, nrt // 2)
        def _(k):
            rt = half * (nrt // 2) + k
            for f in range(fl):
                c = coefficients(f, 3)
                for cb in range(nb):
                    sr, si = slanted(src, 2 * f, c, rt, cb, -1, rows_at)
                    rr, ri = slanted(src, 2 * f + 1, c, rt, cb, -1, rows_at)
                    if keep:
                        dst[2 * f, 0, cb + 2, rows_at(rt)] = sr
                        dst[2 * f, 1, cb + 2, rows_at(rt)] = si
                        dst[2 * f + 1, 0, cb + 2, rows_at(rt)] = rr
                        dst[2 * f + 1, 1, cb + 2, rows_at(rt)] = ri
                    term = sr * rr - si * ri
                    if f > 0:
                        term = tile_load(part, nb, rt, cb) + term
                    tile_store(part, nb, rt, cb, term)

    c_copies = []
    nears = []

    def reduce_chip(t):
        nears[t].wait_recv()
        parts[t, own_half] = parts[t, own_half] + near[t]
        begin(c_copies[t])
        red[t, chip] = parts[t, mine]

    for t in range(steps):
        nears.append(remote(parts.at[t, other_half], near.at[t], near_send.at[t], near_recv.at[t], mate))
        c_copies.append(
            [
                remote(parts.at[t, place(partners[i])], red.at[t, chip], c_send.at[t], c_recv.at[t], partners[i])
                for i in alike
            ]
        )
    for t in range(steps):
        passes[t].wait_recv()
        lens(slabs.at[t], fx, fy)
        rows_then_columns(fy, fx)
        if t + 1 < steps:
            hand_on(t + 1)
        if t > 0:
            reduce_chip(t - 1)
        first_slant(fx, fy)
        second_slant(fy, fx, parts.at[t], t < steps - 1, 1 - side)
        nears[t].start()
        second_slant(fy, fx, parts.at[t], t < steps - 1, side)
    reduce_chip(steps - 1)

    sums = []
    for t in range(steps):
        settle(chips - 1, c_recv.at[t])
        total = red[t, 0]
        for i in range(1, chips):
            total = total + red[t, i]
        sums.append(total / math.sqrt(freq_total))
    d_copies = []
    for i in list(rounds) + [0]:
        k = partners[i]
        value = sums[0] * (owner[0] == k).astype(jnp.float32)
        for t in range(1, steps):
            value = value + sums[t] * (owner[t] == k).astype(jnp.float32)
        if i == 0:
            out[mine] = value
        else:
            image[k] = value
            d_copies.append(remote(image.at[k], out.at[mine], d_send, d_recv, k))
            d_copies[-1].start()
    settle(n - 1, a_send)
    settle(chips - 1, b_send.at[steps - 1])
    for copy in passes + nears:
        copy.wait_send()
    for t in range(steps):
        settle(chips - 1, c_send.at[t])
    settle(n - 1, d_send)
    settle(n - 1, d_recv)


def restore(got, out):
    nb = out.shape[2] // LANE
    for rt in range(out.shape[1] // SUB):
        tiles = deinterleave([tile_load(got, nb, rt, cb) for cb in range(nb)])
        for v in range(nb):
            out[0, rt * SUB : rt * SUB + SUB, v * LANE : v * LANE + LANE] = tiles[v]


def local(n, receiver_data, source_spectrum, filter_taps, slowness, depth_owner, source_position):
    fl, _, height, breadth = receiver_data.shape
    steps = depth_owner.shape[0]
    nb = breadth // LANE
    nrt = height // SUB
    cr = height * nb // n
    slab = slowness[0].reshape(nrt, SUB, nb, LANE).transpose(0, 2, 1, 3).reshape(n, cr, LANE)
    chunks = (n, cr, LANE)
    vmem = pl.BlockSpec(memory_space=pltpu.VMEM)
    hbm = pl.BlockSpec(memory_space=pltpu.HBM)
    fields = (2 * fl, 2, nb + 4, height + 2 * TOP, LANE)
    dma = pltpu.SemaphoreType.DMA
    result = pl.pallas_call(
        functools.partial(kernel, n),
        out_shape=pltpu.VMEM(chunks, jnp.float32),
        in_specs=[hbm] * 6,
        out_specs=vmem,
        scratch_shapes=[
            pltpu.SMEM(depth_owner.shape, jnp.int32),
            pltpu.SMEM(source_position.shape, jnp.int32),
            pltpu.SMEM(source_spectrum.shape, jnp.float32),
            pltpu.SMEM(filter_taps.shape, jnp.float32),
            dma((4,)),
            pltpu.VMEM(receiver_data.shape, jnp.float32),
            pltpu.VMEM(fields, jnp.float32),
            pltpu.VMEM(fields, jnp.float32),
            pltpu.VMEM((fl, 4, 5, SUB, LANE), jnp.float32),
            pltpu.VMEM((fl, 4, SUB, LANE), jnp.float32),
            pltpu.VMEM(chunks, jnp.float32),
            pltpu.VMEM(chunks, jnp.float32),
            pltpu.VMEM(chunks, jnp.float32),
            pltpu.VMEM((steps,) + chunks, jnp.float32),
            pltpu.VMEM((steps,) + chunks, jnp.float32),
            pltpu.VMEM((steps, n // 2, cr, LANE), jnp.float32),
            pltpu.VMEM((steps, n // 2, cr, LANE), jnp.float32),
            pltpu.VMEM(chunks, jnp.float32),
            dma,
            dma,
            dma,
            dma,
            dma((steps,)),
            dma((steps,)),
            dma((steps,)),
            dma((steps,)),
            dma((steps,)),
            dma((steps,)),
            dma((steps,)),
            dma((steps,)),
            dma,
            dma,
        ],
        compiler_params=pltpu.CompilerParams(
            collective_id=0, has_side_effects=True, vmem_limit_bytes=40 * 1024 * 1024
        ),
        name="migrate",
    )(*[pltpu.with_memory_space_constraint(x, pltpu.HBM) for x in (depth_owner, source_position, source_spectrum, filter_taps, receiver_data, slab)])
    return pl.pallas_call(
        restore,
        out_shape=jax.ShapeDtypeStruct((1, height, breadth), jnp.float32),
        in_specs=[vmem],
        out_specs=vmem,
        name="restore",
    )(pltpu.with_memory_space_constraint(result, pltpu.VMEM))


def solution(mesh):
    return jax.shard_map(
        functools.partial(local, mesh.shape["freq"]),
        mesh=mesh,
        in_specs=(
            P(("shot", "freq"), None, None, None),
            P("freq", None),
            P("freq", None, None),
            P("freq", None, None),
            P("shot"),
            P("shot"),
        ),
        out_specs=P(("shot", "freq"), None, None),
        check_vma=False,
    )
```

```python
import functools
import math

import jax
import jax.numpy as jnp
from jax import lax
from jax.experimental import pallas as pl
from jax.experimental.pallas import tpu as pltpu
from jax.sharding import PartitionSpec as P

lens_rate = 3.0
wave_rate = 0.5
middle = 1.25
MESH = pl.DeviceIdType.MESH
SUB = 8
LANE = 128
TOP = 8


def sincos(x):
    k = jnp.floor(x * (2.0 / math.pi) + 0.5)
    r = x - k * 1.5703125
    r = r - k * 4.837512969970703125e-4
    r = r - k * 7.54978995489188216e-8
    q = k.astype(jnp.int32)
    z = r * r
    s = r + r * z * (-1.6666654611e-1 + z * (8.3321608736e-3 - z * 1.9515295891e-4))
    c = 1.0 - 0.5 * z + z * z * (
        4.166664568298827e-2 + z * (-1.388731625493765e-3 + z * 2.443315711809948e-5)
    )
    swap = (q & 1) == 1
    sin = jnp.where(swap, c, s)
    cos = jnp.where(swap, s, c)
    sin = jnp.where((q & 2) == 2, -sin, sin)
    cos = jnp.where(((q + 1) & 2) == 2, -cos, cos)
    return sin, cos


def small_sincos(h):
    z = h * h
    s = h * (1.4142132220 + z * (-0.23569866110 + z * (0.011774833848 + z * -2.6969778329e-4)))
    c = 1.4142135600 + z * (-0.70710668609 + z * (0.058924962733 + z * (-1.9628489073e-3 + z * 3.3861135969e-5)))
    return s * c, 1.0 - s * s


def lane_index():
    return lax.broadcasted_iota(jnp.int32, (SUB, LANE), 1)


def exchanges(nb):
    bits = nb.bit_length() - 1
    pairs, held = [], []
    for k in range(bits):
        at = LANE.bit_length() - 1 + k
        while at >= bits:
            at -= bits
            pairs.append((k, at))
        held.append(at)
    order = [sum((cb >> held[k] & 1) << k for k in range(bits)) for cb in range(nb)]
    return pairs, order


def exchange(tiles, pairs):
    lanes = lane_index()
    tiles = list(tiles)
    for k, at in pairs:
        step = 1 << at
        low = (lanes & step) == 0
        for v in range(len(tiles)):
            if v >> k & 1 == 0:
                w = v + (1 << k)
                a, b = tiles[v], tiles[w]
                tiles[v] = jnp.where(low, a, pltpu.roll(b, step, 1))
                tiles[w] = jnp.where(low, pltpu.roll(a, LANE - step, 1), b)
    return tiles


def interleave(tiles):
    pairs, order = exchanges(len(tiles))
    moved = exchange(tiles, pairs)
    return [moved[v] for v in order]


def deinterleave(tiles):
    pairs, order = exchanges(len(tiles))
    moved = [None] * len(tiles)
    for cb, v in enumerate(order):
        moved[v] = tiles[cb]
    return exchange(moved, pairs[::-1])


def pieces(cr, nb, rt, cb):
    row = cb * SUB
    size = min(cr, SUB)
    return [(rt * (nb * SUB // cr) + (row + o) // cr, (row + o) % cr, size, o) for o in range(0, SUB, size)]


def tile_load(ref, nb, rt, cb):
    got = [ref[c, r : r + m] for c, r, m, _ in pieces(ref.shape[1], nb, rt, cb)]
    return got[0] if len(got) == 1 else jnp.concatenate(got, axis=0)


def tile_store(ref, nb, rt, cb, value):
    for c, r, m, o in pieces(ref.shape[1], nb, rt, cb):
        ref[c, r : r + m] = value[o : o + m]


def kernel(
    n,
    owner_hbm,
    position_hbm,
    spectrum_hbm,
    taps_hbm,
    recv_hbm,
    slow,
    out,
    owner,
    position,
    spectrum,
    taps,
    small_sem,
    rbuf,
    fx,
    fy,
    coefs,
    turns,
    own_slow,
    own_tiles,
    all_slow,
    slabs,
    parts,
    near,
    red,
    image,
    load_sem,
    own_sem,
    a_send,
    a_recv,
    b_send,
    b_recv,
    pass_send,
    pass_recv,
    near_send,
    near_recv,
    c_send,
    c_recv,
    d_send,
    d_recv,
):
    me = lax.axis_index("freq")
    steps = owner.shape[0]
    fl = rbuf.shape[0]
    height = rbuf.shape[2]
    breadth = rbuf.shape[3]
    nb = breadth // LANE
    nrt = height // SUB
    freq_total = n * fl
    first = me * fl

    def peer(i):
        if n & (n - 1):
            return lax.rem(me + i, n)
        to = 0
        for b in range(n.bit_length() - 1):
            bit = lax.rem(lax.div(me, 1 << b), 2)
            to = to + (1 << b) * (1 - bit if i >> b & 1 else bit)
        return to

    partners = [peer(i) for i in range(n)]
    rounds = range(n - 1, 0, -1)
    alike = range(n - 2, 0, -2)
    chips = n // 2
    side = lax.rem(me, 2)
    chip = lax.div(me, 2)
    mate = partners[1]

    def place(device):
        return lax.rem(device, 2) * chips + lax.div(device, 2)

    mine = place(me)
    own_half = pl.ds(side * chips, chips)
    other_half = pl.ds((1 - side) * chips, chips)

    def remote(src, dst, send, recv, to):
        return pltpu.make_async_remote_copy(
            src_ref=src, dst_ref=dst, send_sem=send, recv_sem=recv,
            device_id={"freq": to}, device_id_type=MESH,
        )

    own = pltpu.make_async_copy(slow, own_slow, own_sem)
    own.start()
    barrier = pltpu.get_barrier_semaphore()
    for i in rounds:
        pl.semaphore_signal(barrier, inc=1, device_id={"freq": partners[i]}, device_id_type=MESH)
    load = pltpu.make_async_copy(recv_hbm, rbuf, load_sem)
    load.start()
    small = [
        pltpu.make_async_copy(src, dst, small_sem.at[j])
        for j, (src, dst) in enumerate(
            ((owner_hbm, owner), (position_hbm, position), (spectrum_hbm, spectrum), (taps_hbm, taps))
        )
    ]
    for copy in small:
        copy.start()
    own.wait()
    for rt in range(nrt):
        tiles = interleave([tile_load(own_slow, nb, rt, v) for v in range(nb)])
        for cb in range(nb):
            tile_store(own_tiles, nb, rt, cb, tiles[cb])
    pl.semaphore_wait(barrier, n - 1)

    a_copies = [
        remote(own_tiles.at[place(partners[i])], all_slow.at[me], a_send, a_recv, partners[i])
        for i in rounds
    ]
    for copy in a_copies:
        copy.start()
    all_slow[me] = own_tiles[mine]

    def rows(rt, k=0):
        start = TOP + rt * SUB + k
        return slice(start, start + SUB)

    lanes = lane_index()
    zero = jnp.zeros((SUB, LANE), jnp.float32)

    @pl.loop(0, fl * 2)
    def _(field):
        for part in range(2):
            for cx in range(nb + 4):
                for buf in (fx, fy):
                    buf[field, part, cx, 0:TOP] = zero
                    buf[field, part, cx, TOP + height : 2 * TOP + height] = zero
                    if cx < 2 or cx >= nb + 2:
                        for rt in range(nrt):
                            buf[field, part, cx, rows(rt)] = zero

    for copy in small:
        copy.wait()

    @pl.loop(0, fl)
    def _(f):
        half = jnp.broadcast_to(((first + f).astype(jnp.float32) + 1.0) * (lens_rate / freq_total * 0.5), (SUB, LANE))
        sin, cos = sincos(half * (2.0 * middle))
        turn_re, turn_im = cos, -sin
        for d in range(4):
            c = [jnp.broadcast_to(taps[f, d, j], (SUB, LANE)) for j in range(6)]
            m = jnp.maximum(jnp.abs(c[0]), jnp.abs(c[1]))
            some = m > 0.0
            inverse = 1.0 / jnp.where(some, m, 1.0)
            ur = jnp.where(some, c[0] * inverse, 1.0)
            ui = jnp.where(some, c[1] * inverse, 0.0)
            q = ur * ur + ui * ui
            root = 1.0 / jnp.sqrt(q)
            root = root * (1.5 - 0.5 * q * root * root)
            pr = ur * root
            pi = ui * root
            turn_re, turn_im = turn_re * pr - turn_im * pi, turn_re * pi + turn_im * pr
            coefs[f, d, 0] = m * (q * root)
            for j in (1, 3):
                tr = c[j + 1] * pr + c[j + 2] * pi
                ti = c[j + 2] * pr - c[j + 1] * pi
                coefs[f, d, j] = tr
                coefs[f, d, j + 1] = tr + ti
                coefs[f, d, 5 + j // 2] = ti - tr
        turns[f, 0] = half
        turns[f, 1] = half * middle
        turns[f, 2] = turn_re
        turns[f, 3] = turn_im

    src_row = position[0].astype(jnp.float32)
    src_col = position[1].astype(jnp.float32)
    subs = lax.broadcasted_iota(jnp.int32, (SUB, LANE), 0)
    across = lanes * nb

    @pl.loop(0, nrt)
    def _(rt):
        row = (subs + rt * SUB).astype(jnp.float32) - src_row
        at = pl.ds(pl.multiple_of(TOP + rt * SUB, SUB), SUB)
        for cb in range(nb):
            col = (across + cb).astype(jnp.float32) - src_col
            distance = jnp.sqrt(row * row + col * col + 1.0)
            amplitude = 1.0 / (1.0 + distance / (height / 4.0))
            for f in range(fl):
                number = ((first + f).astype(jnp.float32) + 1.0) * (wave_rate / freq_total)
                sin, cos = sincos(number * distance)
                base_re = amplitude * cos
                base_im = -amplitude * sin
                wr = spectrum[f, 0]
                wi = spectrum[f, 1]
                fx[2 * f, 0, cb + 2, at] = wr * base_re - wi * base_im
                fx[2 * f, 1, cb + 2, at] = wr * base_im + wi * base_re

    load.wait()

    @pl.loop(0, fl)
    def _(f):
        for part in range(2):
            for rt in range(nrt):
                tiles = interleave(
                    [rbuf[f, part, rt * SUB : rt * SUB + SUB, v * LANE : v * LANE + LANE] for v in range(nb)]
                )
                for cb in range(nb):
                    fx[2 * f + 1, part, cb + 2, rows(rt)] = tiles[cb] if part == 0 else -tiles[cb]

    def settle(count, sem):
        space = all_slow.at[0:count]
        pltpu.make_async_copy(space, space, sem).wait()

    settle(n - 1, a_recv)
    b_copies = []
    passes = []
    for t in range(steps):
        slabs[t, mine] = all_slow[owner[t]]
        b_copies.append(
            [
                remote(slabs.at[t, mine], slabs.at[t, mine], b_send.at[t], b_recv.at[t], partners[i])
                for i in alike
            ]
        )
        passes.append(remote(slabs.at[t, own_half], slabs.at[t, own_half], pass_send.at[t], pass_recv.at[t], mate))

    def begin(copies):
        for copy in copies:
            copy.start()

    def hand_on(t):
        settle(chips - 1, b_recv.at[t])
        passes[t].start()

    begin(b_copies[0])
    for t in range(1, steps):
        settle(chips - 1, b_send.at[t - 1])
        begin(b_copies[t])
    hand_on(0)

    edges_first = [0, 1, nb - 2, nb - 1] + list(range(2, nb - 2))

    def combine(c, x, one, two):
        (xr, xi), (pr, pi), (qr, qi) = x, one, two
        both = c[1] * (pr + pi) + c[3] * (qr + qi)
        re = (c[0] * xr + both) - (c[2] * pi + c[4] * qi)
        im = (c[0] * xi + both) + (c[5] * pr + c[6] * qr)
        return re, im

    def coefficients(f, d):
        return [coefs[f, d, j] for j in range(7)]

    def put(dst, field, rt, got):
        for p in range(2):
            for cb in got:
                dst[field, p, cb + 2, rows(rt)] = got[cb][p]
            for k in range(2):
                pltpu.store(
                    dst.at[field, p, nb + 2 + k, rows(rt)], pltpu.roll(got[k][p], LANE - 1, 1), mask=lanes < LANE - 1
                )
                pltpu.store(dst.at[field, p, k, rows(rt)], pltpu.roll(got[nb - 2 + k][p], 1, 1), mask=lanes > 0)

    def lens(slow_now, src, dst):
        @pl.loop(0, fl)
        def _(f):
            half, shift, turn_re, turn_im = (turns[f, j] for j in range(4))
            for rt in range(nrt):
                for cb in range(nb):
                    sin, cos = small_sincos(half * tile_load(slow_now, nb, rt, cb) - shift)
                    fr = cos * turn_re + sin * turn_im
                    fi = cos * turn_im - sin * turn_re
                    for s in range(2):
                        re = src[2 * f + s, 0, cb + 2, rows(rt)]
                        im = src[2 * f + s, 1, cb + 2, rows(rt)]
                        dst[2 * f + s, 0, cb + 2, rows(rt)] = re * fr - im * fi
                        dst[2 * f + s, 1, cb + 2, rows(rt)] = re * fi + im * fr

    def filtered(src, field, c, rt, cb, way, rows=rows):
        down, across = way
        x = [src[field, p, cb + 2, rows(rt)] for p in range(2)]
        one, two = (
            [
                src[field, p, cb + 2 + k * across, rows(rt, k * down)]
                + src[field, p, cb + 2 - k * across, rows(rt, -k * down)]
                for p in range(2)
            ]
            for k in (1, 2)
        )
        return combine(c, x, one, two)

    def direction(src, dst, d, way):
        @pl.loop(0, fl)
        def _(f):
            c = coefficients(f, d)
            for s in range(2):
                for rt in range(nrt):
                    put(dst, 2 * f + s, rt, {cb: filtered(src, 2 * f + s, c, rt, cb, way) for cb in edges_first})

    def rows_at(rt, k=0):
        return pl.ds(pl.multiple_of(TOP + rt * SUB, SUB) + k, SUB)

    def last_direction(src, dst, part, keep, half):
        @pl.loop(0, nrt // 2)
        def _(k):
            rt = half * (nrt // 2) + k
            for f in range(fl):
                c = coefficients(f, 3)
                for cb in range(nb):
                    sr, si = filtered(src, 2 * f, c, rt, cb, (1, -1), rows_at)
                    rr, ri = filtered(src, 2 * f + 1, c, rt, cb, (1, -1), rows_at)
                    if keep:
                        dst[2 * f, 0, cb + 2, rows_at(rt)] = sr
                        dst[2 * f, 1, cb + 2, rows_at(rt)] = si
                        dst[2 * f + 1, 0, cb + 2, rows_at(rt)] = rr
                        dst[2 * f + 1, 1, cb + 2, rows_at(rt)] = ri
                    term = sr * rr - si * ri
                    if f > 0:
                        term = tile_load(part, nb, rt, cb) + term
                    tile_store(part, nb, rt, cb, term)

    c_copies = []
    nears = []

    def reduce_chip(t):
        nears[t].wait_recv()
        parts[t, own_half] = parts[t, own_half] + near[t]
        begin(c_copies[t])
        red[t, chip] = parts[t, mine]

    for t in range(steps):
        nears.append(remote(parts.at[t, other_half], near.at[t], near_send.at[t], near_recv.at[t], mate))
        c_copies.append(
            [
                remote(parts.at[t, place(partners[i])], red.at[t, chip], c_send.at[t], c_recv.at[t], partners[i])
                for i in alike
            ]
        )
    now, then = fx, fy
    for t in range(steps):
        passes[t].wait_recv()
        lens(slabs.at[t], now, then)
        direction(then, now, 0, (1, 0))
        direction(now, then, 1, (0, 1))
        if t + 1 < steps:
            hand_on(t + 1)
        if t > 0:
            reduce_chip(t - 1)
        direction(then, now, 2, (1, 1))
        last_direction(now, then, parts.at[t], t < steps - 1, 1 - side)
        nears[t].start()
        last_direction(now, then, parts.at[t], t < steps - 1, side)
        now, then = then, now
    reduce_chip(steps - 1)

    sums = []
    for t in range(steps):
        settle(chips - 1, c_recv.at[t])
        total = red[t, 0]
        for i in range(1, chips):
            total = total + red[t, i]
        sums.append(total / math.sqrt(freq_total))
    d_copies = []
    for i in list(rounds) + [0]:
        k = partners[i]
        value = sums[0] * (owner[0] == k).astype(jnp.float32)
        for t in range(1, steps):
            value = value + sums[t] * (owner[t] == k).astype(jnp.float32)
        if i == 0:
            out[mine] = value
        else:
            image[k] = value
            d_copies.append(remote(image.at[k], out.at[mine], d_send, d_recv, k))
            d_copies[-1].start()
    settle(n - 1, a_send)
    settle(chips - 1, b_send.at[steps - 1])
    for copy in passes + nears:
        copy.wait_send()
    for t in range(steps):
        settle(chips - 1, c_send.at[t])
    settle(n - 1, d_send)
    settle(n - 1, d_recv)


def restore(got, out):
    nb = out.shape[2] // LANE
    for rt in range(out.shape[1] // SUB):
        tiles = deinterleave([tile_load(got, nb, rt, cb) for cb in range(nb)])
        for v in range(nb):
            out[0, rt * SUB : rt * SUB + SUB, v * LANE : v * LANE + LANE] = tiles[v]


def local(n, receiver_data, source_spectrum, filter_taps, slowness, depth_owner, source_position):
    fl, _, height, breadth = receiver_data.shape
    steps = depth_owner.shape[0]
    nb = breadth // LANE
    nrt = height // SUB
    cr = height * nb // n
    slab = slowness[0].reshape(nrt, SUB, nb, LANE).transpose(0, 2, 1, 3).reshape(n, cr, LANE)
    chunks = (n, cr, LANE)
    vmem = pl.BlockSpec(memory_space=pltpu.VMEM)
    hbm = pl.BlockSpec(memory_space=pltpu.HBM)
    fields = (2 * fl, 2, nb + 4, height + 2 * TOP, LANE)
    dma = pltpu.SemaphoreType.DMA
    result = pl.pallas_call(
        functools.partial(kernel, n),
        out_shape=pltpu.VMEM(chunks, jnp.float32),
        in_specs=[hbm] * 6,
        out_specs=vmem,
        scratch_shapes=[
            pltpu.SMEM(depth_owner.shape, jnp.int32),
            pltpu.SMEM(source_position.shape, jnp.int32),
            pltpu.SMEM(source_spectrum.shape, jnp.float32),
            pltpu.SMEM(filter_taps.shape, jnp.float32),
            dma((4,)),
            pltpu.VMEM(receiver_data.shape, jnp.float32),
            pltpu.VMEM(fields, jnp.float32),
            pltpu.VMEM(fields, jnp.float32),
            pltpu.VMEM((fl, 4, 7, SUB, LANE), jnp.float32),
            pltpu.VMEM((fl, 4, SUB, LANE), jnp.float32),
            pltpu.VMEM(chunks, jnp.float32),
            pltpu.VMEM(chunks, jnp.float32),
            pltpu.VMEM(chunks, jnp.float32),
            pltpu.VMEM((steps,) + chunks, jnp.float32),
            pltpu.VMEM((steps,) + chunks, jnp.float32),
            pltpu.VMEM((steps, n // 2, cr, LANE), jnp.float32),
            pltpu.VMEM((steps, n // 2, cr, LANE), jnp.float32),
            pltpu.VMEM(chunks, jnp.float32),
            dma,
            dma,
            dma,
            dma,
            dma((steps,)),
            dma((steps,)),
            dma((steps,)),
            dma((steps,)),
            dma((steps,)),
            dma((steps,)),
            dma((steps,)),
            dma((steps,)),
            dma,
            dma,
        ],
        compiler_params=pltpu.CompilerParams(
            collective_id=0, has_side_effects=True, vmem_limit_bytes=40 * 1024 * 1024
        ),
        name="migrate",
    )(*[pltpu.with_memory_space_constraint(x, pltpu.HBM) for x in (depth_owner, source_position, source_spectrum, filter_taps, receiver_data, slab)])
    return pl.pallas_call(
        restore,
        out_shape=jax.ShapeDtypeStruct((1, height, breadth), jnp.float32),
        in_specs=[vmem],
        out_specs=vmem,
        name="restore",
    )(pltpu.with_memory_space_constraint(result, pltpu.VMEM))


def solution(mesh):
    return jax.shard_map(
        functools.partial(local, mesh.shape["freq"]),
        mesh=mesh,
        in_specs=(
            P(("shot", "freq"), None, None, None),
            P("freq", None),
            P("freq", None, None),
            P("freq", None, None),
            P("shot"),
            P("shot"),
        ),
        out_specs=P(("shot", "freq"), None, None),
        check_vma=False,
    )
```

```python
import functools
import math

import jax
import jax.numpy as jnp
from jax import lax
from jax.experimental import pallas as pl
from jax.experimental.pallas import tpu as pltpu
from jax.sharding import PartitionSpec as P

lens_rate = 3.0
wave_rate = 0.5
middle = 1.25
MESH = pl.DeviceIdType.MESH
SUB = 8
LANE = 128
TOP = 8


def sincos(x):
    k = jnp.floor(x * (2.0 / math.pi) + 0.5)
    r = x - k * 1.5703125
    r = r - k * 4.837512969970703125e-4
    r = r - k * 7.54978995489188216e-8
    q = k.astype(jnp.int32)
    z = r * r
    s = r + r * z * (-1.6666654611e-1 + z * (8.3321608736e-3 - z * 1.9515295891e-4))
    c = 1.0 - 0.5 * z + z * z * (
        4.166664568298827e-2 + z * (-1.388731625493765e-3 + z * 2.443315711809948e-5)
    )
    swap = (q & 1) == 1
    sin = jnp.where(swap, c, s)
    cos = jnp.where(swap, s, c)
    sin = jnp.where((q & 2) == 2, -sin, sin)
    cos = jnp.where(((q + 1) & 2) == 2, -cos, cos)
    return sin, cos


def small_sincos(h):
    z = h * h
    s = h * (1.4142132220 + z * (-0.23569866110 + z * (0.011774833848 + z * -2.6969778329e-4)))
    c = 1.4142135600 + z * (-0.70710668609 + z * (0.058924962733 + z * (-1.9628489073e-3 + z * 3.3861135969e-5)))
    return s * c, 1.0 - s * s


def lane_index():
    return lax.broadcasted_iota(jnp.int32, (SUB, LANE), 1)


def exchanges(nb):
    bits = nb.bit_length() - 1
    pairs, held = [], []
    for k in range(bits):
        at = LANE.bit_length() - 1 + k
        while at >= bits:
            at -= bits
            pairs.append((k, at))
        held.append(at)
    order = [sum((cb >> held[k] & 1) << k for k in range(bits)) for cb in range(nb)]
    return pairs, order


def exchange(tiles, pairs):
    lanes = lane_index()
    tiles = list(tiles)
    for k, at in pairs:
        step = 1 << at
        low = (lanes & step) == 0
        for v in range(len(tiles)):
            if v >> k & 1 == 0:
                w = v + (1 << k)
                a, b = tiles[v], tiles[w]
                tiles[v] = jnp.where(low, a, pltpu.roll(b, step, 1))
                tiles[w] = jnp.where(low, pltpu.roll(a, LANE - step, 1), b)
    return tiles


def interleave(tiles):
    pairs, order = exchanges(len(tiles))
    moved = exchange(tiles, pairs)
    return [moved[v] for v in order]


def deinterleave(tiles):
    pairs, order = exchanges(len(tiles))
    moved = [None] * len(tiles)
    for cb, v in enumerate(order):
        moved[v] = tiles[cb]
    return exchange(moved, pairs[::-1])


def pieces(cr, nb, rt, cb):
    row = cb * SUB
    size = min(cr, SUB)
    return [(rt * (nb * SUB // cr) + (row + o) // cr, (row + o) % cr, size, o) for o in range(0, SUB, size)]


def tile_load(ref, nb, rt, cb):
    got = [ref[c, r : r + m] for c, r, m, _ in pieces(ref.shape[1], nb, rt, cb)]
    return got[0] if len(got) == 1 else jnp.concatenate(got, axis=0)


def tile_store(ref, nb, rt, cb, value):
    for c, r, m, o in pieces(ref.shape[1], nb, rt, cb):
        ref[c, r : r + m] = value[o : o + m]


def kernel(
    n,
    owner_hbm,
    position_hbm,
    spectrum_hbm,
    taps_hbm,
    recv_hbm,
    slow,
    out,
    owner,
    position,
    spectrum,
    taps,
    small_sem,
    rbuf,
    fx,
    fy,
    coefs,
    turns,
    own_slow,
    own_tiles,
    all_slow,
    slabs,
    parts,
    near,
    red,
    image,
    load_sem,
    own_sem,
    a_send,
    a_recv,
    b_send,
    b_recv,
    pass_send,
    pass_recv,
    near_send,
    near_recv,
    c_send,
    c_recv,
    d_send,
    d_recv,
):
    me = lax.axis_index("freq")
    steps = owner.shape[0]
    fl = rbuf.shape[0]
    height = rbuf.shape[2]
    breadth = rbuf.shape[3]
    nb = breadth // LANE
    nrt = height // SUB
    freq_total = n * fl
    first = me * fl

    def peer(i):
        if n & (n - 1):
            return lax.rem(me + i, n)
        to = 0
        for b in range(n.bit_length() - 1):
            bit = lax.rem(lax.div(me, 1 << b), 2)
            to = to + (1 << b) * (1 - bit if i >> b & 1 else bit)
        return to

    partners = [peer(i) for i in range(n)]
    rounds = range(n - 1, 0, -1)
    alike = range(n - 2, 0, -2)
    chips = n // 2
    side = lax.rem(me, 2)
    chip = lax.div(me, 2)
    mate = partners[1]

    def place(device):
        return lax.rem(device, 2) * chips + lax.div(device, 2)

    mine = place(me)
    own_half = pl.ds(side * chips, chips)
    other_half = pl.ds((1 - side) * chips, chips)

    def remote(src, dst, send, recv, to):
        return pltpu.make_async_remote_copy(
            src_ref=src, dst_ref=dst, send_sem=send, recv_sem=recv,
            device_id={"freq": to}, device_id_type=MESH,
        )

    own = pltpu.make_async_copy(slow, own_slow, own_sem)
    own.start()
    barrier = pltpu.get_barrier_semaphore()
    for i in rounds:
        pl.semaphore_signal(barrier, inc=1, device_id={"freq": partners[i]}, device_id_type=MESH)
    load = pltpu.make_async_copy(recv_hbm, rbuf, load_sem)
    load.start()
    small = [
        pltpu.make_async_copy(src, dst, small_sem.at[j])
        for j, (src, dst) in enumerate(
            ((owner_hbm, owner), (position_hbm, position), (spectrum_hbm, spectrum), (taps_hbm, taps))
        )
    ]
    for copy in small:
        copy.start()
    own.wait()
    for rt in range(nrt):
        tiles = interleave([tile_load(own_slow, nb, rt, v) for v in range(nb)])
        for cb in range(nb):
            tile_store(own_tiles, nb, rt, cb, tiles[cb])
    pl.semaphore_wait(barrier, n - 1)

    a_copies = [
        remote(own_tiles.at[place(partners[i])], all_slow.at[me], a_send, a_recv, partners[i])
        for i in rounds
    ]
    for copy in a_copies:
        copy.start()
    all_slow[me] = own_tiles[mine]

    def rows(rt, k=0):
        start = TOP + rt * SUB + k
        return slice(start, start + SUB)

    lanes = lane_index()
    zero = jnp.zeros((SUB, LANE), jnp.float32)

    @pl.loop(0, fl * 2)
    def _(field):
        for part in range(2):
            for cx in range(nb + 4):
                for buf in (fx, fy):
                    buf[field, part, cx, 0:TOP] = zero
                    buf[field, part, cx, TOP + height : 2 * TOP + height] = zero
                    if cx < 2 or cx >= nb + 2:
                        for rt in range(nrt):
                            buf[field, part, cx, rows(rt)] = zero

    for copy in small:
        copy.wait()

    @pl.loop(0, fl)
    def _(f):
        half = jnp.broadcast_to(((first + f).astype(jnp.float32) + 1.0) * (lens_rate / freq_total * 0.5), (SUB, LANE))
        sin, cos = sincos(half * (2.0 * middle))
        turn_re, turn_im = cos, -sin
        for d in range(4):
            c = [jnp.broadcast_to(taps[f, d, j], (SUB, LANE)) for j in range(6)]
            m = jnp.maximum(jnp.abs(c[0]), jnp.abs(c[1]))
            some = m > 0.0
            inverse = 1.0 / jnp.where(some, m, 1.0)
            ur = jnp.where(some, c[0] * inverse, 1.0)
            ui = jnp.where(some, c[1] * inverse, 0.0)
            q = ur * ur + ui * ui
            root = 1.0 / jnp.sqrt(q)
            root = root * (1.5 - 0.5 * q * root * root)
            pr = ur * root
            pi = ui * root
            turn_re, turn_im = turn_re * pr - turn_im * pi, turn_re * pi + turn_im * pr
            coefs[f, d, 0] = m * (q * root)
            for j in (1, 3):
                tr = c[j + 1] * pr + c[j + 2] * pi
                ti = c[j + 2] * pr - c[j + 1] * pi
                coefs[f, d, j] = tr
                coefs[f, d, j + 1] = tr + ti
                coefs[f, d, 5 + j // 2] = ti - tr
        turns[f, 0] = half
        turns[f, 1] = half * middle
        turns[f, 2] = turn_re
        turns[f, 3] = turn_im

    src_row = position[0].astype(jnp.float32)
    src_col = position[1].astype(jnp.float32)
    subs = lax.broadcasted_iota(jnp.int32, (SUB, LANE), 0)
    across = lanes * nb

    @pl.loop(0, nrt)
    def _(rt):
        row = (subs + rt * SUB).astype(jnp.float32) - src_row
        at = pl.ds(pl.multiple_of(TOP + rt * SUB, SUB), SUB)
        for cb in range(nb):
            col = (across + cb).astype(jnp.float32) - src_col
            distance = jnp.sqrt(row * row + col * col + 1.0)
            amplitude = 1.0 / (1.0 + distance / (height / 4.0))
            for f in range(fl):
                number = ((first + f).astype(jnp.float32) + 1.0) * (wave_rate / freq_total)
                sin, cos = sincos(number * distance)
                base_re = amplitude * cos
                base_im = -amplitude * sin
                wr = spectrum[f, 0]
                wi = spectrum[f, 1]
                fx[2 * f, 0, cb + 2, at] = wr * base_re - wi * base_im
                fx[2 * f, 1, cb + 2, at] = wr * base_im + wi * base_re

    load.wait()

    @pl.loop(0, fl)
    def _(f):
        for part in range(2):
            for rt in range(nrt):
                tiles = interleave(
                    [rbuf[f, part, rt * SUB : rt * SUB + SUB, v * LANE : v * LANE + LANE] for v in range(nb)]
                )
                for cb in range(nb):
                    fx[2 * f + 1, part, cb + 2, rows(rt)] = tiles[cb] if part == 0 else -tiles[cb]

    def settle(count, sem):
        space = all_slow.at[0:count]
        pltpu.make_async_copy(space, space, sem).wait()

    settle(n - 1, a_recv)
    b_copies = []
    passes = []
    for t in range(steps):
        slabs[t, mine] = all_slow[owner[t]]
        b_copies.append(
            [
                remote(slabs.at[t, mine], slabs.at[t, mine], b_send.at[t], b_recv.at[t], partners[i])
                for i in alike
            ]
        )
        passes.append(remote(slabs.at[t, own_half], slabs.at[t, own_half], pass_send.at[t], pass_recv.at[t], mate))

    def begin(copies):
        for copy in copies:
            copy.start()

    def hand_on(t):
        settle(chips - 1, b_recv.at[t])
        passes[t].start()

    begin(b_copies[0])
    for t in range(1, steps):
        settle(chips - 1, b_send.at[t - 1])
        begin(b_copies[t])
    hand_on(0)

    edges_first = [0, 1, nb - 2, nb - 1] + list(range(2, nb - 2))

    def combine(c, x, one, two):
        (xr, xi), (pr, pi), (qr, qi) = x, one, two
        both = c[1] * (pr + pi) + c[3] * (qr + qi)
        re = (c[0] * xr + both) - (c[2] * pi + c[4] * qi)
        im = (c[0] * xi + both) + (c[5] * pr + c[6] * qr)
        return re, im

    def coefficients(f, d):
        return [coefs[f, d, j] for j in range(7)]

    def put(dst, field, rt, got):
        for p in range(2):
            for cb in got:
                dst[field, p, cb + 2, rows(rt)] = got[cb][p]
            for k in range(2):
                pltpu.store(
                    dst.at[field, p, nb + 2 + k, rows(rt)], pltpu.roll(got[k][p], LANE - 1, 1), mask=lanes < LANE - 1
                )
                pltpu.store(dst.at[field, p, k, rows(rt)], pltpu.roll(got[nb - 2 + k][p], 1, 1), mask=lanes > 0)

    def rows_at(rt, k=0):
        return pl.ds(pl.multiple_of(TOP + rt * SUB, SUB) + k, SUB)

    def lens(slow_now, src, dst, half):
        @pl.loop(0, nrt // 2)
        def _(k):
            rt = half * (nrt // 2) + k
            for f in range(fl):
                span, shift, turn_re, turn_im = (turns[f, j] for j in range(4))
                for cb in range(nb):
                    sin, cos = small_sincos(span * tile_load(slow_now, nb, rt, cb) - shift)
                    fr = cos * turn_re + sin * turn_im
                    fi = cos * turn_im - sin * turn_re
                    for s in range(2):
                        re = src[2 * f + s, 0, cb + 2, rows_at(rt)]
                        im = src[2 * f + s, 1, cb + 2, rows_at(rt)]
                        dst[2 * f + s, 0, cb + 2, rows_at(rt)] = re * fr - im * fi
                        dst[2 * f + s, 1, cb + 2, rows_at(rt)] = re * fi + im * fr

    def filtered(src, field, c, rt, cb, way, rows=rows):
        down, across = way
        x = [src[field, p, cb + 2, rows(rt)] for p in range(2)]
        one, two = (
            [
                src[field, p, cb + 2 + k * across, rows(rt, k * down)]
                + src[field, p, cb + 2 - k * across, rows(rt, -k * down)]
                for p in range(2)
            ]
            for k in (1, 2)
        )
        return combine(c, x, one, two)

    def direction(src, dst, d, way):
        @pl.loop(0, fl)
        def _(f):
            c = coefficients(f, d)
            for s in range(2):
                for rt in range(nrt):
                    put(dst, 2 * f + s, rt, {cb: filtered(src, 2 * f + s, c, rt, cb, way) for cb in edges_first})

    def last_direction(src, dst, part, keep, half):
        @pl.loop(0, nrt // 2)
        def _(k):
            rt = half * (nrt // 2) + k
            for f in range(fl):
                c = coefficients(f, 3)
                for cb in range(nb):
                    sr, si = filtered(src, 2 * f, c, rt, cb, (1, -1), rows_at)
                    rr, ri = filtered(src, 2 * f + 1, c, rt, cb, (1, -1), rows_at)
                    if keep:
                        dst[2 * f, 0, cb + 2, rows_at(rt)] = sr
                        dst[2 * f, 1, cb + 2, rows_at(rt)] = si
                        dst[2 * f + 1, 0, cb + 2, rows_at(rt)] = rr
                        dst[2 * f + 1, 1, cb + 2, rows_at(rt)] = ri
                    term = sr * rr - si * ri
                    if f > 0:
                        term = tile_load(part, nb, rt, cb) + term
                    tile_store(part, nb, rt, cb, term)

    c_copies = []
    nears = []

    def reduce_chip(t):
        nears[t].wait_recv()
        parts[t, own_half] = parts[t, own_half] + near[t]
        begin(c_copies[t])
        red[t, chip] = parts[t, mine]

    for t in range(steps):
        nears.append(remote(parts.at[t, other_half], near.at[t], near_send.at[t], near_recv.at[t], mate))
        c_copies.append(
            [
                remote(parts.at[t, place(partners[i])], red.at[t, chip], c_send.at[t], c_recv.at[t], partners[i])
                for i in alike
            ]
        )
    now, then = fx, fy
    for t in range(steps):
        lens(slabs.at[t], now, then, side)
        passes[t].wait_recv()
        lens(slabs.at[t], now, then, 1 - side)
        direction(then, now, 0, (1, 0))
        direction(now, then, 1, (0, 1))
        if t + 1 < steps:
            hand_on(t + 1)
        if t > 0:
            reduce_chip(t - 1)
        direction(then, now, 2, (1, 1))
        last_direction(now, then, parts.at[t], t < steps - 1, 1 - side)
        nears[t].start()
        last_direction(now, then, parts.at[t], t < steps - 1, side)
        now, then = then, now
    reduce_chip(steps - 1)

    sums = []
    for t in range(steps):
        settle(chips - 1, c_recv.at[t])
        total = red[t, 0]
        for i in range(1, chips):
            total = total + red[t, i]
        sums.append(total / math.sqrt(freq_total))
    d_copies = []
    for i in list(rounds) + [0]:
        k = partners[i]
        value = sums[0] * (owner[0] == k).astype(jnp.float32)
        for t in range(1, steps):
            value = value + sums[t] * (owner[t] == k).astype(jnp.float32)
        if i == 0:
            out[mine] = value
        else:
            image[k] = value
            d_copies.append(remote(image.at[k], out.at[mine], d_send, d_recv, k))
            d_copies[-1].start()
    settle(n - 1, a_send)
    settle(chips - 1, b_send.at[steps - 1])
    for copy in passes + nears:
        copy.wait_send()
    for t in range(steps):
        settle(chips - 1, c_send.at[t])
    settle(n - 1, d_send)
    settle(n - 1, d_recv)


def restore(got, out):
    nb = out.shape[2] // LANE
    for rt in range(out.shape[1] // SUB):
        tiles = deinterleave([tile_load(got, nb, rt, cb) for cb in range(nb)])
        for v in range(nb):
            out[0, rt * SUB : rt * SUB + SUB, v * LANE : v * LANE + LANE] = tiles[v]


def local(n, receiver_data, source_spectrum, filter_taps, slowness, depth_owner, source_position):
    fl, _, height, breadth = receiver_data.shape
    steps = depth_owner.shape[0]
    nb = breadth // LANE
    nrt = height // SUB
    cr = height * nb // n
    slab = slowness[0].reshape(nrt, SUB, nb, LANE).transpose(0, 2, 1, 3).reshape(n, cr, LANE)
    chunks = (n, cr, LANE)
    vmem = pl.BlockSpec(memory_space=pltpu.VMEM)
    hbm = pl.BlockSpec(memory_space=pltpu.HBM)
    fields = (2 * fl, 2, nb + 4, height + 2 * TOP, LANE)
    dma = pltpu.SemaphoreType.DMA
    result = pl.pallas_call(
        functools.partial(kernel, n),
        out_shape=pltpu.VMEM(chunks, jnp.float32),
        in_specs=[hbm] * 6,
        out_specs=vmem,
        scratch_shapes=[
            pltpu.SMEM(depth_owner.shape, jnp.int32),
            pltpu.SMEM(source_position.shape, jnp.int32),
            pltpu.SMEM(source_spectrum.shape, jnp.float32),
            pltpu.SMEM(filter_taps.shape, jnp.float32),
            dma((4,)),
            pltpu.VMEM(receiver_data.shape, jnp.float32),
            pltpu.VMEM(fields, jnp.float32),
            pltpu.VMEM(fields, jnp.float32),
            pltpu.VMEM((fl, 4, 7, SUB, LANE), jnp.float32),
            pltpu.VMEM((fl, 4, SUB, LANE), jnp.float32),
            pltpu.VMEM(chunks, jnp.float32),
            pltpu.VMEM(chunks, jnp.float32),
            pltpu.VMEM(chunks, jnp.float32),
            pltpu.VMEM((steps,) + chunks, jnp.float32),
            pltpu.VMEM((steps,) + chunks, jnp.float32),
            pltpu.VMEM((steps, n // 2, cr, LANE), jnp.float32),
            pltpu.VMEM((steps, n // 2, cr, LANE), jnp.float32),
            pltpu.VMEM(chunks, jnp.float32),
            dma,
            dma,
            dma,
            dma,
            dma((steps,)),
            dma((steps,)),
            dma((steps,)),
            dma((steps,)),
            dma((steps,)),
            dma((steps,)),
            dma((steps,)),
            dma((steps,)),
            dma,
            dma,
        ],
        compiler_params=pltpu.CompilerParams(
            collective_id=0, has_side_effects=True, vmem_limit_bytes=40 * 1024 * 1024
        ),
        name="migrate",
    )(*[pltpu.with_memory_space_constraint(x, pltpu.HBM) for x in (depth_owner, source_position, source_spectrum, filter_taps, receiver_data, slab)])
    return pl.pallas_call(
        restore,
        out_shape=jax.ShapeDtypeStruct((1, height, breadth), jnp.float32),
        in_specs=[vmem],
        out_specs=vmem,
        name="restore",
    )(pltpu.with_memory_space_constraint(result, pltpu.VMEM))


def solution(mesh):
    return jax.shard_map(
        functools.partial(local, mesh.shape["freq"]),
        mesh=mesh,
        in_specs=(
            P(("shot", "freq"), None, None, None),
            P("freq", None),
            P("freq", None, None),
            P("freq", None, None),
            P("shot"),
            P("shot"),
        ),
        out_specs=P(("shot", "freq"), None, None),
        check_vma=False,
    )
```

```python
import functools
import math

import jax
import jax.numpy as jnp
from jax import lax
from jax.experimental import pallas as pl
from jax.experimental.pallas import tpu as pltpu
from jax.sharding import PartitionSpec as P

lens_rate = 3.0
wave_rate = 0.5
middle = 1.25
MESH = pl.DeviceIdType.MESH
SUB = 8
LANE = 128
TOP = 8


def sincos(x):
    k = jnp.floor(x * (2.0 / math.pi) + 0.5)
    r = x - k * 1.5703125
    r = r - k * 4.837512969970703125e-4
    r = r - k * 7.54978995489188216e-8
    q = k.astype(jnp.int32)
    z = r * r
    s = r + r * z * (-1.6666654611e-1 + z * (8.3321608736e-3 - z * 1.9515295891e-4))
    c = 1.0 - 0.5 * z + z * z * (
        4.166664568298827e-2 + z * (-1.388731625493765e-3 + z * 2.443315711809948e-5)
    )
    swap = (q & 1) == 1
    sin = jnp.where(swap, c, s)
    cos = jnp.where(swap, s, c)
    sin = jnp.where((q & 2) == 2, -sin, sin)
    cos = jnp.where(((q + 1) & 2) == 2, -cos, cos)
    return sin, cos


def small_sincos(h):
    z = h * h
    s = h * (1.4142132220 + z * (-0.23569866110 + z * (0.011774833848 + z * -2.6969778329e-4)))
    c = 1.4142135600 + z * (-0.70710668609 + z * (0.058924962733 + z * (-1.9628489073e-3 + z * 3.3861135969e-5)))
    return s * c, 1.0 - s * s


def lane_index():
    return lax.broadcasted_iota(jnp.int32, (SUB, LANE), 1)


def exchanges(nb):
    bits = nb.bit_length() - 1
    pairs, held = [], []
    for k in range(bits):
        at = LANE.bit_length() - 1 + k
        while at >= bits:
            at -= bits
            pairs.append((k, at))
        held.append(at)
    order = [sum((cb >> held[k] & 1) << k for k in range(bits)) for cb in range(nb)]
    return pairs, order


def exchange(tiles, pairs):
    lanes = lane_index()
    tiles = list(tiles)
    for k, at in pairs:
        step = 1 << at
        low = (lanes & step) == 0
        for v in range(len(tiles)):
            if v >> k & 1 == 0:
                w = v + (1 << k)
                a, b = tiles[v], tiles[w]
                tiles[v] = jnp.where(low, a, pltpu.roll(b, step, 1))
                tiles[w] = jnp.where(low, pltpu.roll(a, LANE - step, 1), b)
    return tiles


def interleave(tiles):
    pairs, order = exchanges(len(tiles))
    moved = exchange(tiles, pairs)
    return [moved[v] for v in order]


def deinterleave(tiles):
    pairs, order = exchanges(len(tiles))
    moved = [None] * len(tiles)
    for cb, v in enumerate(order):
        moved[v] = tiles[cb]
    return exchange(moved, pairs[::-1])


def pieces(cr, nb, rt, cb):
    row = cb * SUB
    size = min(cr, SUB)
    return [(rt * (nb * SUB // cr) + (row + o) // cr, (row + o) % cr, size, o) for o in range(0, SUB, size)]


def tile_load(ref, nb, rt, cb):
    got = [ref[c, r : r + m] for c, r, m, _ in pieces(ref.shape[1], nb, rt, cb)]
    return got[0] if len(got) == 1 else jnp.concatenate(got, axis=0)


def tile_store(ref, nb, rt, cb, value):
    for c, r, m, o in pieces(ref.shape[1], nb, rt, cb):
        ref[c, r : r + m] = value[o : o + m]


def kernel(
    n,
    owner_hbm,
    position_hbm,
    spectrum_hbm,
    taps_hbm,
    recv_hbm,
    slow,
    out,
    owner,
    position,
    spectrum,
    taps,
    small_sem,
    rbuf,
    fx,
    fy,
    coefs,
    turns,
    own_slow,
    own_tiles,
    all_slow,
    slabs,
    parts,
    near,
    red,
    image,
    load_sem,
    own_sem,
    a_send,
    a_recv,
    b_send,
    b_recv,
    pass_send,
    pass_recv,
    near_send,
    near_recv,
    c_send,
    c_recv,
    d_send,
    d_recv,
):
    me = lax.axis_index("freq")
    steps = owner.shape[0]
    fl = rbuf.shape[0]
    height = rbuf.shape[2]
    breadth = rbuf.shape[3]
    nb = breadth // LANE
    nrt = height // SUB
    freq_total = n * fl
    first = me * fl

    def peer(i):
        if n & (n - 1):
            return lax.rem(me + i, n)
        to = 0
        for b in range(n.bit_length() - 1):
            bit = lax.rem(lax.div(me, 1 << b), 2)
            to = to + (1 << b) * (1 - bit if i >> b & 1 else bit)
        return to

    partners = [peer(i) for i in range(n)]
    rounds = range(n - 1, 0, -1)
    alike = range(n - 2, 0, -2)
    chips = n // 2
    side = lax.rem(me, 2)
    chip = lax.div(me, 2)
    mate = partners[1]

    def place(device):
        return lax.rem(device, 2) * chips + lax.div(device, 2)

    mine = place(me)
    own_half = pl.ds(side * chips, chips)
    other_half = pl.ds((1 - side) * chips, chips)

    def remote(src, dst, send, recv, to):
        return pltpu.make_async_remote_copy(
            src_ref=src, dst_ref=dst, send_sem=send, recv_sem=recv,
            device_id={"freq": to}, device_id_type=MESH,
        )

    own = pltpu.make_async_copy(slow, own_slow, own_sem)
    own.start()
    barrier = pltpu.get_barrier_semaphore()
    for i in rounds:
        pl.semaphore_signal(barrier, inc=1, device_id={"freq": partners[i]}, device_id_type=MESH)
    load = pltpu.make_async_copy(recv_hbm, rbuf, load_sem)
    load.start()
    small = [
        pltpu.make_async_copy(src, dst, small_sem.at[j])
        for j, (src, dst) in enumerate(
            ((owner_hbm, owner), (position_hbm, position), (spectrum_hbm, spectrum), (taps_hbm, taps))
        )
    ]
    for copy in small:
        copy.start()
    own.wait()
    for rt in range(nrt):
        tiles = interleave([tile_load(own_slow, nb, rt, v) for v in range(nb)])
        for cb in range(nb):
            tile_store(own_tiles, nb, rt, cb, tiles[cb])
    pl.semaphore_wait(barrier, n - 1)

    a_copies = [
        remote(own_tiles.at[place(partners[i])], all_slow.at[me], a_send, a_recv, partners[i])
        for i in rounds
    ]
    for copy in a_copies:
        copy.start()
    all_slow[me] = own_tiles[mine]

    def rows(rt, k=0):
        start = TOP + rt * SUB + k
        return slice(start, start + SUB)

    lanes = lane_index()
    zero = jnp.zeros((SUB, LANE), jnp.float32)

    @pl.loop(0, fl * 2)
    def _(field):
        for part in range(2):
            for cx in range(nb + 4):
                for buf in (fx, fy):
                    buf[field, part, cx, 0:TOP] = zero
                    buf[field, part, cx, TOP + height : 2 * TOP + height] = zero
                    if cx < 2 or cx >= nb + 2:
                        for rt in range(nrt):
                            buf[field, part, cx, rows(rt)] = zero

    for copy in small:
        copy.wait()

    @pl.loop(0, fl)
    def _(f):
        half = jnp.broadcast_to(((first + f).astype(jnp.float32) + 1.0) * (lens_rate / freq_total * 0.5), (SUB, LANE))
        sin, cos = sincos(half * (2.0 * middle))
        turn_re, turn_im = cos, -sin
        for d in range(4):
            c = [jnp.broadcast_to(taps[f, d, j], (SUB, LANE)) for j in range(6)]
            m = jnp.maximum(jnp.abs(c[0]), jnp.abs(c[1]))
            some = m > 0.0
            inverse = 1.0 / jnp.where(some, m, 1.0)
            ur = jnp.where(some, c[0] * inverse, 1.0)
            ui = jnp.where(some, c[1] * inverse, 0.0)
            q = ur * ur + ui * ui
            root = 1.0 / jnp.sqrt(q)
            root = root * (1.5 - 0.5 * q * root * root)
            pr = ur * root
            pi = ui * root
            turn_re, turn_im = turn_re * pr - turn_im * pi, turn_re * pi + turn_im * pr
            coefs[f, d, 0] = m * (q * root)
            for j in (1, 3):
                tr = c[j + 1] * pr + c[j + 2] * pi
                ti = c[j + 2] * pr - c[j + 1] * pi
                coefs[f, d, j] = tr
                coefs[f, d, j + 1] = tr + ti
                coefs[f, d, 5 + j // 2] = ti - tr
        turns[f, 0] = half
        turns[f, 1] = half * middle
        turns[f, 2] = turn_re
        turns[f, 3] = turn_im

    src_row = position[0].astype(jnp.float32)
    src_col = position[1].astype(jnp.float32)
    subs = lax.broadcasted_iota(jnp.int32, (SUB, LANE), 0)
    across = lanes * nb

    @pl.loop(0, nrt)
    def _(rt):
        row = (subs + rt * SUB).astype(jnp.float32) - src_row
        at = pl.ds(pl.multiple_of(TOP + rt * SUB, SUB), SUB)
        for cb in range(nb):
            col = (across + cb).astype(jnp.float32) - src_col
            distance = jnp.sqrt(row * row + col * col + 1.0)
            amplitude = 1.0 / (1.0 + distance / (height / 4.0))
            for f in range(fl):
                number = ((first + f).astype(jnp.float32) + 1.0) * (wave_rate / freq_total)
                sin, cos = sincos(number * distance)
                base_re = amplitude * cos
                base_im = -amplitude * sin
                wr = spectrum[f, 0]
                wi = spectrum[f, 1]
                fx[2 * f, 0, cb + 2, at] = wr * base_re - wi * base_im
                fx[2 * f, 1, cb + 2, at] = wr * base_im + wi * base_re

    load.wait()

    @pl.loop(0, fl)
    def _(f):
        for part in range(2):
            for rt in range(nrt):
                tiles = interleave(
                    [rbuf[f, part, rt * SUB : rt * SUB + SUB, v * LANE : v * LANE + LANE] for v in range(nb)]
                )
                for cb in range(nb):
                    fx[2 * f + 1, part, cb + 2, rows(rt)] = tiles[cb] if part == 0 else -tiles[cb]

    def settle(count, sem):
        space = all_slow.at[0:count]
        pltpu.make_async_copy(space, space, sem).wait()

    settle(n - 1, a_recv)
    b_copies = []
    passes = []
    for t in range(steps):
        slabs[t, mine] = all_slow[owner[t]]
        b_copies.append(
            [
                remote(slabs.at[t, mine], slabs.at[t, mine], b_send.at[t], b_recv.at[t], partners[i])
                for i in alike
            ]
        )
        passes.append(remote(slabs.at[t, own_half], slabs.at[t, own_half], pass_send.at[t], pass_recv.at[t], mate))

    def begin(copies):
        for copy in copies:
            copy.start()

    def hand_on(t):
        settle(chips - 1, b_recv.at[t])
        passes[t].start()

    begin(b_copies[0])
    for t in range(1, steps):
        settle(chips - 1, b_send.at[t - 1])
        begin(b_copies[t])
    hand_on(0)

    edges_first = [0, 1, nb - 2, nb - 1] + list(range(2, nb - 2))

    def combine(c, x, one, two):
        (xr, xi), (pr, pi), (qr, qi) = x, one, two
        both = c[1] * (pr + pi) + c[3] * (qr + qi)
        re = (c[0] * xr + both) - (c[2] * pi + c[4] * qi)
        im = (c[0] * xi + both) + (c[5] * pr + c[6] * qr)
        return re, im

    def coefficients(f, d):
        return [coefs[f, d, j] for j in range(7)]

    def put(dst, field, rt, got):
        for p in range(2):
            for cb in got:
                dst[field, p, cb + 2, rows(rt)] = got[cb][p]
            for k in range(2):
                pltpu.store(
                    dst.at[field, p, nb + 2 + k, rows(rt)], pltpu.roll(got[k][p], LANE - 1, 1), mask=lanes < LANE - 1
                )
                pltpu.store(dst.at[field, p, k, rows(rt)], pltpu.roll(got[nb - 2 + k][p], 1, 1), mask=lanes > 0)

    def rows_at(rt, k=0):
        return pl.ds(pl.multiple_of(TOP + rt * SUB, SUB) + k, SUB)

    def lens(slow_now, src, dst, half):
        @pl.loop(0, nrt // 2)
        def _(k):
            rt = half * (nrt // 2) + k
            for f in range(fl):
                span, shift, turn_re, turn_im = (turns[f, j] for j in range(4))
                for cb in range(nb):
                    sin, cos = small_sincos(span * tile_load(slow_now, nb, rt, cb) - shift)
                    fr = cos * turn_re + sin * turn_im
                    fi = cos * turn_im - sin * turn_re
                    for s in range(2):
                        re = src[2 * f + s, 0, cb + 2, rows_at(rt)]
                        im = src[2 * f + s, 1, cb + 2, rows_at(rt)]
                        dst[2 * f + s, 0, cb + 2, rows_at(rt)] = re * fr - im * fi
                        dst[2 * f + s, 1, cb + 2, rows_at(rt)] = re * fi + im * fr

    def filtered(src, field, c, rt, cb, way, rows=rows):
        down, across = way
        x = [src[field, p, cb + 2, rows(rt)] for p in range(2)]
        one, two = (
            [
                src[field, p, cb + 2 + k * across, rows(rt, k * down)]
                + src[field, p, cb + 2 - k * across, rows(rt, -k * down)]
                for p in range(2)
            ]
            for k in (1, 2)
        )
        return combine(c, x, one, two)

    def direction(src, dst, d, way):
        @pl.loop(0, fl)
        def _(f):
            c = coefficients(f, d)
            for s in range(2):
                for rt in range(nrt):
                    put(dst, 2 * f + s, rt, {cb: filtered(src, 2 * f + s, c, rt, cb, way) for cb in edges_first})

    def last_direction(src, dst, part, keep, half):
        @pl.loop(0, nrt // 2)
        def _(k):
            rt = half * (nrt // 2) + k
            for cb in range(nb):
                total = None
                for f in range(fl):
                    c = coefficients(f, 3)
                    sr, si = filtered(src, 2 * f, c, rt, cb, (1, -1), rows_at)
                    rr, ri = filtered(src, 2 * f + 1, c, rt, cb, (1, -1), rows_at)
                    if keep:
                        dst[2 * f, 0, cb + 2, rows_at(rt)] = sr
                        dst[2 * f, 1, cb + 2, rows_at(rt)] = si
                        dst[2 * f + 1, 0, cb + 2, rows_at(rt)] = rr
                        dst[2 * f + 1, 1, cb + 2, rows_at(rt)] = ri
                    term = sr * rr - si * ri
                    total = term if total is None else total + term
                tile_store(part, nb, rt, cb, total)

    c_copies = []
    nears = []

    def reduce_chip(t):
        nears[t].wait_recv()
        parts[t, own_half] = parts[t, own_half] + near[t]
        begin(c_copies[t])
        red[t, chip] = parts[t, mine]

    for t in range(steps):
        nears.append(remote(parts.at[t, other_half], near.at[t], near_send.at[t], near_recv.at[t], mate))
        c_copies.append(
            [
                remote(parts.at[t, place(partners[i])], red.at[t, chip], c_send.at[t], c_recv.at[t], partners[i])
                for i in alike
            ]
        )
    now, then = fx, fy
    for t in range(steps):
        lens(slabs.at[t], now, then, side)
        passes[t].wait_recv()
        lens(slabs.at[t], now, then, 1 - side)
        direction(then, now, 0, (1, 0))
        direction(now, then, 1, (0, 1))
        if t + 1 < steps:
            hand_on(t + 1)
        if t > 0:
            reduce_chip(t - 1)
        direction(then, now, 2, (1, 1))
        last_direction(now, then, parts.at[t], t < steps - 1, 1 - side)
        nears[t].start()
        last_direction(now, then, parts.at[t], t < steps - 1, side)
        now, then = then, now
    reduce_chip(steps - 1)

    def total_of(t):
        settle(chips - 1, c_recv.at[t])
        total = red[t, 0]
        for i in range(1, chips):
            total = total + red[t, i]
        return total / math.sqrt(freq_total)

    sums = [total_of(t) for t in range(steps - 1)]
    for k in range(n):
        value = jnp.zeros_like(image[k])
        for t in range(steps - 1):
            value = value + sums[t] * (owner[t] == k).astype(jnp.float32)
        image[k] = value
    settle(n - 1, a_send)
    settle(chips - 1, b_send.at[steps - 1])
    for copy in passes + nears:
        copy.wait_send()
    for t in range(steps - 1):
        settle(chips - 1, c_send.at[t])
    newest = total_of(steps - 1)
    for k in [partners[i] for i in rounds]:
        image[k] = image[k] + newest * (owner[steps - 1] == k).astype(jnp.float32)
        remote(image.at[k], out.at[mine], d_send, d_recv, k).start()
    out[mine] = image[me] + newest * (owner[steps - 1] == me).astype(jnp.float32)
    settle(chips - 1, c_send.at[steps - 1])
    settle(n - 1, d_send)
    settle(n - 1, d_recv)


def restore(got, out):
    nb = out.shape[2] // LANE
    for rt in range(out.shape[1] // SUB):
        tiles = deinterleave([tile_load(got, nb, rt, cb) for cb in range(nb)])
        for v in range(nb):
            out[0, rt * SUB : rt * SUB + SUB, v * LANE : v * LANE + LANE] = tiles[v]


def local(n, receiver_data, source_spectrum, filter_taps, slowness, depth_owner, source_position):
    fl, _, height, breadth = receiver_data.shape
    steps = depth_owner.shape[0]
    nb = breadth // LANE
    nrt = height // SUB
    cr = height * nb // n
    slab = slowness[0].reshape(nrt, SUB, nb, LANE).transpose(0, 2, 1, 3).reshape(n, cr, LANE)
    chunks = (n, cr, LANE)
    vmem = pl.BlockSpec(memory_space=pltpu.VMEM)
    hbm = pl.BlockSpec(memory_space=pltpu.HBM)
    fields = (2 * fl, 2, nb + 4, height + 2 * TOP, LANE)
    dma = pltpu.SemaphoreType.DMA
    result = pl.pallas_call(
        functools.partial(kernel, n),
        out_shape=pltpu.VMEM(chunks, jnp.float32),
        in_specs=[hbm] * 6,
        out_specs=vmem,
        scratch_shapes=[
            pltpu.SMEM(depth_owner.shape, jnp.int32),
            pltpu.SMEM(source_position.shape, jnp.int32),
            pltpu.SMEM(source_spectrum.shape, jnp.float32),
            pltpu.SMEM(filter_taps.shape, jnp.float32),
            dma((4,)),
            pltpu.VMEM(receiver_data.shape, jnp.float32),
            pltpu.VMEM(fields, jnp.float32),
            pltpu.VMEM(fields, jnp.float32),
            pltpu.VMEM((fl, 4, 7, SUB, LANE), jnp.float32),
            pltpu.VMEM((fl, 4, SUB, LANE), jnp.float32),
            pltpu.VMEM(chunks, jnp.float32),
            pltpu.VMEM(chunks, jnp.float32),
            pltpu.VMEM(chunks, jnp.float32),
            pltpu.VMEM((steps,) + chunks, jnp.float32),
            pltpu.VMEM((steps,) + chunks, jnp.float32),
            pltpu.VMEM((steps, n // 2, cr, LANE), jnp.float32),
            pltpu.VMEM((steps, n // 2, cr, LANE), jnp.float32),
            pltpu.VMEM(chunks, jnp.float32),
            dma,
            dma,
            dma,
            dma,
            dma((steps,)),
            dma((steps,)),
            dma((steps,)),
            dma((steps,)),
            dma((steps,)),
            dma((steps,)),
            dma((steps,)),
            dma((steps,)),
            dma,
            dma,
        ],
        compiler_params=pltpu.CompilerParams(
            collective_id=0, has_side_effects=True, vmem_limit_bytes=40 * 1024 * 1024
        ),
        name="migrate",
    )(*[pltpu.with_memory_space_constraint(x, pltpu.HBM) for x in (depth_owner, source_position, source_spectrum, filter_taps, receiver_data, slab)])
    return pl.pallas_call(
        restore,
        out_shape=jax.ShapeDtypeStruct((1, height, breadth), jnp.float32),
        in_specs=[vmem],
        out_specs=vmem,
        name="restore",
    )(pltpu.with_memory_space_constraint(result, pltpu.VMEM))


def solution(mesh):
    return jax.shard_map(
        functools.partial(local, mesh.shape["freq"]),
        mesh=mesh,
        in_specs=(
            P(("shot", "freq"), None, None, None),
            P("freq", None),
            P("freq", None, None),
            P("freq", None, None),
            P("shot"),
            P("shot"),
        ),
        out_specs=P(("shot", "freq"), None, None),
        check_vma=False,
    )
```
